32 devices in a mesh: parts: 2 (over x), wide: 16 (over z, y, core).
Axes of the slice: x: 2, y: 2, z: 4, core: 2. Of those that a mesh axis runs over, the one named last changes fastest.
Arguments:
- tokens: bfloat16 [384, 7168], P(('parts', 'wide')), parts along dimension 0, may hold values from -6 to 6
- expert_ids: int32 [384, 8], P(('parts', 'wide')), parts along dimension 0, may hold values from 0 to 15, as said below
- gates: float32 [384, 8], P(('parts', 'wide')), parts along dimension 0, may hold values from 0.1 to 1
- w_gate: bfloat16 [2, 7168, 8192], P(None, None, 'wide'), may hold values from -0.0625 to 0.0625
- w_up: bfloat16 [2, 7168, 8192], P(None, None, 'wide'), may hold values from -0.0625 to 0.0625
- w_down: bfloat16 [2, 8192, 7168], P(None, 'wide'), may hold values from -0.1875 to 0.1875
Outputs:
- moe_out: bfloat16 [384, 7168], P(('parts', 'wide')), parts along dimension 0
The draws below stay inside these ranges and needn't reach their ends.
There are 2 independent parts, one for each index of `parts`. The reference program is written for one: setup_inputs(seed, part) draws one part's arguments, and reference() takes and returns one part's arrays. A program takes and returns all parts, laid end to end along the dimension named above; an argument that names none is the same for every part. Nothing has to cross between parts.
Inputs may be any that keep to these rules, and one draw needn't show every extreme that they name: `expert_ids`: each row names the 2 experts g * 2 to g * 2 + 1 of each of 4 different groups g, in any order; in each part one group is named by every row.
All inputs are finite; a program needn't handle non-finite values.
Results may differ from the reference program's by a relative error of at most 0.0064.
Values may be sent and summed in bfloat16 or wider, within the bound.
A program may use at most 128 MiB of HBM per device.

```python
import jax
import jax.numpy as jnp
from jax import lax

D = 7168
GROUPS = 8
TOPG = 4
TOPK = 8
EXP_G = 2
FH = 1024
TOKENS = 192
EXPERTS = 16
N_WIDE = 16


def draw_expert_ids(key, part):
    key_hot, key_group, key_order = jax.random.split(jax.random.fold_in(key, 7103), 3)
    hot_group = jax.random.randint(key_hot, (), 0, GROUPS)
    group_range = jnp.arange(GROUPS, dtype=jnp.int32)
    noise = jax.random.randint(key_group, (TOKENS, GROUPS), 0, 1 << 20)
    scores = noise * GROUPS + group_range[None, :]
    scores = jnp.where(group_range[None, :] == hot_group, -1, scores)
    chosen_groups = jnp.argsort(scores, axis=1, stable=True)[:, :TOPG]
    experts_named = (chosen_groups[:, :, None] * EXP_G + jnp.arange(EXP_G, dtype=jnp.int32)[None, None, :]).reshape(TOKENS, TOPK)
    order_noise = jax.random.randint(key_order, (TOKENS, TOPK), 0, 1 << 20) * TOPK + jnp.arange(TOPK, dtype=jnp.int32)[None, :]
    shuffle = jnp.argsort(order_noise, axis=1, stable=True)
    return jnp.take_along_axis(experts_named, shuffle, axis=1).astype(jnp.int32)


def block_scale(stream_key, dims, cuts, least, top_value):
    factor_of, own = 1.0, jax.random.fold_in(stream_key, 6)
    for axis_at, parts in cuts:
        heights = jnp.exp(jax.random.uniform(jax.random.fold_in(own, axis_at), (parts,), jnp.float32, least / len(cuts), top_value / len(cuts)))
        factor_of = factor_of * jnp.repeat(heights, dims[axis_at] // parts).reshape([-1 if axis == axis_at else 1 for axis in range(len(dims))])
    return factor_of


def centred(key, shape, spread, limit, pieces=(), kind=jnp.bfloat16):
    result = jax.random.normal(key, shape, jnp.float32) * spread
    if len(pieces) > 0:
        result = block_scale(key, shape, pieces, -0.22, 0.18) * result
    return jnp.clip(result, min=-limit, max=limit).astype(kind)


def setup_inputs(seed: int = 0, part: int = 0) -> dict:
    keys = jax.random.split(jax.random.key(seed), 7)
    part_keys = jax.random.split(jax.random.fold_in(keys[6], part), 7)
    return {
        "tokens": centred(part_keys[0], (TOKENS, D), 1.0, 6.0, ((0, 16),)),
        "expert_ids": draw_expert_ids(jax.random.fold_in(jax.random.fold_in(keys[6], part), 71), part),
        "gates": jnp.clip(0.1 + 0.9 * jax.random.uniform(part_keys[2], (TOKENS, TOPK), jnp.float32) ** block_scale(part_keys[2], (TOKENS, TOPK), ((0, 16),), -0.2, 0.2), 0.1, 1.0),
        "w_gate": centred(keys[3], (EXP_G, D, GROUPS * FH), D ** -0.5, 0.0625, ((2, 16),)),
        "w_up": centred(keys[4], (EXP_G, D, GROUPS * FH), D ** -0.5, 0.0625, ((2, 16),)),
        "w_down": centred(keys[5], (EXP_G, GROUPS * FH, D), FH ** -0.5, 0.1875, ((1, 16),)),
    }


def reference(tokens, expert_ids, gates, w_gate, w_up, w_down):
    group_size = N_WIDE // GROUPS
    block_width = FH // group_size
    catalog = jnp.arange(EXPERTS, dtype=jnp.int32)
    picked = expert_ids[:, :, None] == catalog[None, None, :]
    route_weight = jnp.sum(jnp.where(picked, gates[:, :, None], jnp.float32(0.0)), axis=1).astype(jnp.bfloat16)

    def add_block(device, summed):
        device = jnp.asarray(device).astype(jnp.int32)
        group_index = device // group_size
        column_start = (device * block_width).astype(jnp.int32)
        gate_block = lax.dynamic_slice_in_dim(w_gate, column_start, block_width, 2)
        up_block = lax.dynamic_slice_in_dim(w_up, column_start, block_width, 2)
        down_block = lax.dynamic_slice_in_dim(w_down, column_start, block_width, 1)
        scales = lax.dynamic_slice_in_dim(route_weight, (group_index * EXP_G).astype(jnp.int32), EXP_G, 1).astype(jnp.float32)
        partial_value = jnp.zeros((TOKENS, D), jnp.float32)
        for expert in range(EXP_G):
            gate_value = jnp.dot(tokens, gate_block[expert], preferred_element_type=jnp.float32)
            lifted = jnp.dot(tokens, up_block[expert], preferred_element_type=jnp.float32)
            hidden = (jax.nn.silu(gate_value) * lifted).astype(jnp.bfloat16)
            partial_value = partial_value + scales[:, expert:expert + 1] * jnp.dot(hidden, down_block[expert], preferred_element_type=jnp.float32)
        rounded = lax.optimization_barrier(partial_value.astype(jnp.bfloat16))
        return summed + rounded.astype(jnp.float32)

    summed = lax.fori_loop(0, N_WIDE, add_block, jnp.zeros((TOKENS, D), jnp.float32))
    return summed.astype(jnp.bfloat16)
```

```python
import functools
import math

import jax
import jax.numpy as jnp
from jax import lax
from jax.experimental import pallas as pl
from jax.experimental.pallas import tpu as pltpu
from jax.sharding import PartitionSpec as P

GROUPS = 8
EXP_G = 2
CORES = 2
SIDES = 2
LANES = 128
CHUNK = 256
BATCHES = 1
SPLIT = 0
AHEAD = 20
SPLIT_AHEAD = 0
LAG_RELAY = 0
LAG_SIDE = 2
LAG_USE = 3
LAG_SUM = 2
LAG_Z = 5
LAG_ZR = 5
LAG_END = 8
NEAR = 3
F32 = jnp.float32
BF16 = jnp.bfloat16


def floor_div(value, by):
    return jnp.floor((value + 0.5) * (1.0 / by))


def iota_f32(shape, dim):
    return lax.broadcasted_iota(jnp.int32, shape, dim).astype(F32)


def one_hot(match):
    return match.astype(F32).astype(BF16)


def kernel(
    wide, rows, batches, fold, split,
    tok_ref, ids_ref, gate_ref, wg_ref, wu_ref, wd_ref, out_ref,
    tok, padded, r_ref, xb, rb, wb, wdb, acc, hid, perm, perm_back, packed, got_core, red, got_side, got_z, relay, got_y, fin,
    tok_sem, own_sem, w_sem, d_sem, route_s, route_r, out_s, az_r, af_r, ay_r, ac_r, bc_r, by_r, bz_r, br_r,
):
    zs = wide // (CORES * SIDES)
    total = xb.shape[0]
    chunks = total // batches
    hidden = wg_ref.shape[2]
    part = rows // batches
    unit = part * fold
    span = fold * CHUNK
    units = wide
    groups = units // fold
    size = fold * unit
    lines = units * part
    pad_rows = r_ref.shape[0]
    near = range(1, min(NEAR, zs - 1) + 1)
    far = range(NEAR + 1, zs)
    extra = batches * split

    me = lax.axis_index("wide")
    core = lax.rem(me, CORES)
    chip = me // CORES
    side = lax.rem(chip, SIDES)
    z = chip // SIDES
    other_core = 1 - core
    other_side = 1 - side
    halves = (side, other_side)

    def at(z_at, side_at, core_at):
        return {"wide": (z_at * SIDES + side_at) * CORES + core_at}

    core_dev = at(z, side, other_core)
    side_dev = at(z, other_side, core)

    def inside(value):
        return (value >= 0) & (value < zs)

    def around(distances):
        return [(d, sign, z + sign * d, (d - 1) * 2 + (sign + 1) // 2) for d in distances for sign in (-1, 1)]

    def send(src, dst, s_sem, r_sem, dev):
        return pltpu.make_async_remote_copy(
            src_ref=src, dst_ref=dst, send_sem=s_sem, recv_sem=r_sem, device_id=dev, device_id_type=pl.DeviceIdType.MESH
        )

    def up_copies(k):
        rows_of = pl.ds(pl.multiple_of(k * span, span), span)
        return [
            pltpu.make_async_copy(wg_ref.at[:, rows_of, :], wb.at[k, pl.ds(0, EXP_G)], w_sem.at[k]),
            pltpu.make_async_copy(wu_ref.at[:, rows_of, :], wb.at[k, pl.ds(EXP_G, EXP_G)], w_sem.at[k]),
        ]

    def up_wait(k):
        pltpu.make_async_copy(wb.at[k], wb.at[k], w_sem.at[k]).wait()

    def down_copies(k):
        columns = pl.ds(pl.multiple_of(k * span, span), span)
        return [
            pltpu.make_async_copy(wd_ref.at[e, :, columns], wdb.at[k, pl.ds(e * hidden, hidden), :], d_sem.at[k])
            for e in range(EXP_G)
        ]

    def down_wait(k):
        pltpu.make_async_copy(wdb.at[k], wdb.at[k], d_sem.at[k]).wait()

    def line_of(q, rel, first):
        return q if rel == 0 else total + q // chunks * split + lax.rem(q, chunks) - first

    def by_count(pairs, rule, act):
        here = sum(rule(z + sign * d, z - sign).astype(jnp.int32) for d, sign in pairs)
        held_here = {sum(bool(rule(spot + sign * d, spot - sign)) for d, sign in pairs) for spot in range(zs)}
        for n in sorted(held_here - {0}):
            @pl.when(here == n)
            def _():
                act(n)

    def ends(distances):
        return [(d, sign) for d in distances for sign in (-1, 1)]

    def any_end(value, behind):
        return inside(value)

    def any_through(value, behind):
        return inside(value) & inside(behind)

    def any_first(value, behind):
        return inside(value) & ((behind < 0) | (behind >= zs))

    def z_hop(q, rel, src, dst, kind, r_sem):
        spot = xb.at[q, core, halves[rel], src]
        return send(spot, spot, out_s.at[kind], r_sem, at(dst, side, core))

    def y_hop(q, half, src, kind):
        spot = xb.at[q, core, half, src]
        return send(spot, spot, out_s.at[kind], ay_r.at[q], side_dev)

    def core_hop(q, owner, rel):
        spot = xb.at[q, owner, halves[rel]]
        return send(spot, spot, out_s.at[6], ac_r.at[q], core_dev)

    def z_own(q, rel):
        line = line_of(q, rel, chunks - split)
        for d, sign, dst, slot in reversed(around(near)):
            @pl.when(inside(dst))
            def _():
                z_hop(q, rel, z, dst, rel, az_r.at[line, slot]).start()

    def z_onward(q, rel, distances, onward):
        for d, sign, src, slot in around(distances):
            @pl.when(inside(src))
            def _():
                if d >= NEAR and d + 1 < zs:
                    @pl.when(inside(z - sign))
                    def _():
                        z_hop(q, rel, src, z - sign, 2 + rel, af_r.at[line_of(q, rel, chunks - split), d - NEAR]).start()
                if onward:
                    y_hop(q, side, src, 5).start()

    def z_wait(q, rel, distances, r_sem):
        def wait(n):
            spot = xb.at[q, core, halves[rel], pl.ds(0, n)]
            send(spot, spot, out_s.at[0], r_sem, core_dev).wait_recv()

        by_count(ends(distances), any_end, wait)

    def arrive_near(q, rel, onward):
        line = line_of(q, rel, chunks - split)
        for d, sign, src, slot in around(near):
            @pl.when(inside(z - sign * d))
            def _():
                z_hop(q, rel, z - sign * d, z - sign * d, 0, az_r.at[line, slot]).wait_recv()
                if d >= NEAR and d + 1 < zs:
                    @pl.when(inside(z + sign))
                    def _():
                        z_hop(q, rel, z - sign * d, z + sign, 2 + rel, af_r.at[line, d - NEAR]).start()
                if onward:
                    y_hop(q, side, z - sign * d, 5).start()

    def arrive_far(q, rel, onward):
        for d in far:
            z_wait(q, rel, [d], af_r.at[line_of(q, rel, chunks - split), d - NEAR - 1])
            z_onward(q, rel, [d], onward)

    def route_z(step):
        dst = lax.rem(z + step, zs)
        return send(r_ref, rb.at[core, side, z], route_s.at[0], route_r.at[step], at(dst, side, core))

    def route_side(half):
        return send(rb.at[core, half], rb.at[core, half], route_s.at[1], route_r.at[zs], side_dev)

    def route_core(owner):
        return send(rb.at[owner], rb.at[owner], route_s.at[2], route_r.at[zs + 1], core_dev)

    def route_local():
        return pltpu.make_async_copy(r_ref, rb.at[core, side, z], own_sem)

    def back_core(p):
        return send(packed.at[p, other_core], got_core.at[p], out_s.at[7], bc_r.at[p], core_dev)

    def back_side(p):
        return send(red.at[p, 1], got_side.at[p], out_s.at[8], by_r.at[p], side_dev)

    def back_last(p):
        return send(got_y.at[p, 0], got_y.at[p, 1], out_s.at[9], by_r.at[p], side_dev)

    def back_z(p, rel, dst, slot):
        r_sem = bz_r.at[line_of(p, rel, 0)]
        return send(red.at[p, rel, dst], got_z.at[p, rel, slot], out_s.at[10 + rel], r_sem, at(dst, side, core))

    def back_relay(p, rel, d, dst, to):
        r_sem = br_r.at[line_of(p, rel, 0), d]
        return send(red.at[p, rel, dst], relay.at[p, rel, dst], out_s.at[12 + rel], r_sem, at(to, side, core))

    def reduce_out(p, rel, d, sign, dst, slot):
        if d <= NEAR:
            back_z(p, rel, dst, slot).start()
        else:
            back_relay(p, rel, d - NEAR - 1, dst, z + sign).start()

    def reduce_first(p, rel):
        for d, sign, dst, slot in reversed(around(range(1, zs))):
            ready = inside(dst) if d < NEAR else any_first(dst, z - sign)

            @pl.when(ready)
            def _():
                reduce_out(p, rel, d, sign, dst, slot)

    def reduce_second(p, rel):
        for d in reversed(range(NEAR, zs - 1)):
            def wait(n):
                spot = relay.at[p, rel, pl.ds(0, n)]
                send(spot, spot, out_s.at[0], br_r.at[line_of(p, rel, 0), d - NEAR], core_dev).wait_recv()

            by_count(ends([d]), any_through, wait)
            for _, sign, dst, slot in around([d]):
                @pl.when(any_through(dst, z - sign))
                def _():
                    red[p, rel, dst] = (red[p, rel, dst].astype(F32) + relay[p, rel, dst].astype(F32)).astype(BF16)
                    reduce_out(p, rel, d, sign, dst, slot)

    def reduce_last(p, rel):
        def wait(n):
            spot = got_z.at[p, rel, pl.ds(0, n)]
            send(spot, spot, out_s.at[0], bz_r.at[line_of(p, rel, 0)], core_dev).wait_recv()

        by_count(ends(near), any_end, wait)
        done = red[p, rel, z].astype(F32)
        for d, sign, src, slot in around(near):
            done = done + got_z[p, rel, slot].astype(F32)
        return done

    token_copy = pltpu.make_async_copy(tok_ref, tok, tok_sem)
    token_copy.start()
    for copy in up_copies(0):
        copy.start()

    for d, sign, src, slot in around(near):
        @pl.when(jnp.logical_not(inside(z - sign * d)))
        def _():
            @pl.loop(0, total)
            def _(p):
                for rel in range(SIDES):
                    got_z[p, rel, slot] = jnp.zeros((unit, CHUNK), BF16)

    barrier = pltpu.get_barrier_semaphore()
    for step in range(1, zs):
        pl.semaphore_signal(barrier, inc=1, device_id=at(lax.rem(z + step, zs), side, core), device_id_type=pl.DeviceIdType.MESH)
    pl.semaphore_signal(barrier, inc=1, device_id=side_dev, device_id_type=pl.DeviceIdType.MESH)
    pl.semaphore_signal(barrier, inc=1, device_id=core_dev, device_id_type=pl.DeviceIdType.MESH)

    def place(index):
        batch = floor_div(index, unit)
        rest = index - batch * unit
        block = floor_div(rest, part)
        return block * pad_rows + batch * part + rest - block * part

    held = batches * unit
    into = one_hot(iota_f32((held, fold * pad_rows), 1) == place(iota_f32((held, 1), 0)))
    spread = one_hot(iota_f32((pad_rows, rows), 0) == iota_f32((pad_rows, rows), 1))
    token_copy.wait()
    padded[...] = jnp.dot(spread, tok[...], preferred_element_type=F32).astype(BF16)

    def pack(k):
        tiles = jnp.concatenate([padded[:, k * span + f * CHUNK:k * span + (f + 1) * CHUNK] for f in range(fold)], axis=0)
        mine = jnp.dot(into, tiles, preferred_element_type=F32).astype(BF16)
        for b in range(batches):
            xb[b * chunks + k, core, side, z] = mine[b * unit:(b + 1) * unit]

    def offer(q):
        y_hop(q, side, z, 4).start()
        z_own(q, 0)

    token = lax.broadcasted_iota(jnp.int32, (LANES, rows), 0)
    route = jnp.zeros((LANES, rows), F32)
    for slot in range(ids_ref.shape[0]):
        route = route + jnp.where(ids_ref[slot:slot + 1, :] == token, gate_ref[slot:slot + 1, :], 0.0)
    r_ref[...] = lax.dot_general(spread, route.astype(BF16), (((1,), (1,)), ((), ())), preferred_element_type=F32).astype(BF16)
    route_local().start()
    pack(0)
    pl.semaphore_wait(barrier, zs + 1)
    offer(0)
    for step in range(1, zs):
        route_z(step).start()
    for k in range(1, chunks):
        pack(k)
        if k < AHEAD:
            offer(k)
    for q in range(chunks, min(AHEAD, total)):
        offer(q)

    def order(index):
        first = floor_div(index, unit)
        rest = index - first * unit
        second = floor_div(rest, part)
        return second * unit + first * part + (rest - second * part)

    perm[...] = one_hot(order(iota_f32((size, 1), 0)) == iota_f32((size, size), 1))
    perm_back[...] = one_hot(iota_f32((size, size), 0) == order(iota_f32((1, size), 1)))
    acc[...] = jnp.zeros_like(acc)

    lag_down = LAG_USE + chunks - 1

    def staged(lag, count=total):
        def wrap(body):
            def run(now):
                @pl.when((now >= lag) & (now < count + lag))
                def _():
                    body(now - lag)
            return run
        return wrap

    def either(test, yes, no):
        if split == 0:
            no()
        else:
            pl.when(test)(yes)
            pl.when(jnp.logical_not(test))(no)

    def gather_split(q):
        return lax.rem(q, chunks) >= chunks - split

    def scatter_split(p):
        return lax.rem(p, chunks) < split

    @staged(-AHEAD)
    def stage_offer(q):
        offer(q)

    @staged(0, chunks)
    def stage_weights(k):
        @pl.when(k + 1 < chunks)
        def _():
            for copy in up_copies(k + 1):
                copy.start()

        for copy in down_copies(k):
            copy.start()

    @staged(0)
    def stage_arrive(q):
        def both():
            arrive_near(q, 0, False)
            arrive_near(q, 1, False)

        either(gather_split(q), both, lambda: arrive_near(q, 0, True))

        @pl.when(q == chunks // 2)
        def _():
            route_local().wait()
            for step in range(1, zs):
                route_z(step).wait_recv()
            route_side(side).start()

    @staged(-SPLIT_AHEAD)
    def stage_split(q):
        def both():
            y_hop(q, other_side, z, 4).wait_recv()
            z_own(q, 1)

        either(gather_split(q), both, lambda: None)

    @staged(LAG_RELAY)
    def stage_relay(q):
        def both():
            arrive_far(q, 0, False)
            arrive_far(q, 1, False)
            core_hop(q, core, 0).start()
            core_hop(q, core, 1).start()

        def one():
            arrive_far(q, 0, True)
            core_hop(q, core, 0).start()

        either(gather_split(q), both, one)

    @staged(LAG_SIDE)
    def stage_side(q):
        def one():
            spot = xb.at[q, core, other_side]
            send(spot, spot, out_s.at[5], ay_r.at[q], side_dev).wait_recv()
            core_hop(q, core, 1).start()

        either(gather_split(q), lambda: None, one)

        @pl.when(q == chunks // 2)
        def _():
            route_side(other_side).wait_recv()
            route_core(core).start()

    @staged(LAG_USE)
    def stage_up(q):
        spot = xb.at[q, other_core]
        send(spot, spot, out_s.at[6], ac_r.at[q], core_dev).wait_recv()
        k = lax.rem(q, chunks)

        @pl.when(q < chunks)
        def _():
            up_wait(k)

        folded = xb[q].reshape(groups, size, CHUNK)
        moved = jnp.dot(perm[...], jnp.concatenate([folded[g] for g in range(groups)], axis=1), preferred_element_type=F32).astype(BF16)
        left = jnp.concatenate([
            jnp.concatenate([moved[f * unit:(f + 1) * unit, g * CHUNK:(g + 1) * CHUNK] for f in range(fold)], axis=1)
            for g in range(groups)
        ], axis=0)
        for e in range(EXP_G):
            acc[2 * e] += jnp.dot(left, wb[k, e], preferred_element_type=F32)
            acc[2 * e + 1] += jnp.dot(left, wb[k, EXP_G + e], preferred_element_type=F32)

        @pl.when(k == chunks - 1)
        def _():
            b = q // chunks

            @pl.when(b == 0)
            def _():
                route_core(other_core).wait_recv()

            line = iota_f32((1, units * pad_rows), 1)
            unit_of = floor_div(line, pad_rows)
            row_of = line - unit_of * pad_rows - (b * part).astype(F32)
            wanted = jnp.where((row_of >= 0) & (row_of < part), unit_of * part + row_of, -1.0)
            pick = one_hot(iota_f32((lines, units * pad_rows), 0) == wanted)
            scales = jnp.dot(pick, rb[...].reshape(units * pad_rows, LANES), preferred_element_type=F32)
            lane = lax.broadcasted_iota(jnp.int32, (lines, LANES), 1)
            first_expert = me // (wide // GROUPS) * EXP_G
            for e in range(EXP_G):
                scale = jnp.sum(jnp.where(lane == first_expert + e, scales, 0.0), axis=1, keepdims=True)
                gate = acc[2 * e]
                value = gate / (1.0 + jnp.exp(-gate)) * acc[2 * e + 1]
                hid[b, :, e * hidden:(e + 1) * hidden] = (value * scale).astype(BF16)
            acc[...] = jnp.zeros_like(acc)

    @staged(lag_down)
    def stage_down(p):
        k = lax.rem(p, chunks)

        @pl.when(p < chunks)
        def _():
            down_wait(k)

        down = jnp.dot(hid[p // chunks], wdb[k], preferred_element_type=F32).astype(BF16)
        stacked = jnp.concatenate([
            jnp.concatenate([down[g * unit:(g + 1) * unit, f * CHUNK:(f + 1) * CHUNK] for f in range(fold)], axis=0)
            for g in range(groups)
        ], axis=1)
        moved = jnp.dot(perm_back[...], stacked, preferred_element_type=F32).astype(BF16)
        flat = jnp.concatenate([moved[:, g * CHUNK:(g + 1) * CHUNK] for g in range(groups)], axis=0)
        packed[p] = flat.reshape(CORES, SIDES, zs, unit, CHUNK)
        back_core(p).start()

    @staged(lag_down + LAG_SUM)
    def stage_sum(p):
        back_core(p).wait_recv()
        for rel in (1, 0):
            red[p, rel] = (packed[p, core, halves[rel]].astype(F32) + got_core[p, halves[rel]].astype(F32)).astype(BF16)

        def both():
            reduce_first(p, 0)
            reduce_first(p, 1)

        either(scatter_split(p), both, lambda: back_side(p).start())

    @staged(lag_down + LAG_Z)
    def stage_z(p):
        def both():
            reduce_second(p, 0)
            reduce_second(p, 1)

        def one():
            back_side(p).wait_recv()
            red[p, 0] = (red[p, 0].astype(F32) + got_side[p].astype(F32)).astype(BF16)
            reduce_first(p, 0)

        either(scatter_split(p), both, one)

    @staged(lag_down + LAG_ZR)
    def stage_zr(p):
        def both():
            got_y[p, 0] = reduce_last(p, 1).astype(BF16)
            back_last(p).start()

        either(scatter_split(p), both, lambda: reduce_second(p, 0))

    @staged(lag_down + LAG_END)
    def stage_end(p):
        b = p // chunks
        k = lax.rem(p, chunks)
        spot = pl.ds(pl.multiple_of(b * unit, unit), unit)

        def both():
            back_last(p).wait_recv()
            fin[k, spot] = (reduce_last(p, 0) + got_y[p, 1].astype(F32)).astype(BF16)

        def one():
            fin[k, spot] = reduce_last(p, 0).astype(BF16)

        either(scatter_split(p), both, one)

        @pl.when(b == batches - 1)
        def _():
            out_of = one_hot(iota_f32((fold * pad_rows, held), 0) == place(iota_f32((1, held), 1)))
            flat = jnp.dot(out_of, fin[k], preferred_element_type=F32).astype(BF16)
            for f in range(fold):
                columns = pl.ds(pl.multiple_of(k * span + f * CHUNK, CHUNK), CHUNK)
                out_ref[:, columns] = flat[f * pad_rows:f * pad_rows + rows]

    @pl.loop(0, total + lag_down + LAG_END)
    def _(now):
        stage_weights(now)
        stage_offer(now)
        stage_arrive(now)
        stage_split(now)
        stage_relay(now)
        stage_side(now)
        stage_sum(now)
        stage_z(now)
        stage_zr(now)
        stage_end(now)
        stage_up(now)
        stage_down(now)

    def sent(kind, spot):
        send(spot, spot, out_s.at[kind], ay_r.at[0], core_dev).wait_send()

    plain = total - extra

    def sent_lines(kind, pairs, rule, ref):
        by_count(pairs, rule, lambda n: sent(kind, ref.at[:, 0, pl.ds(0, n)]))
        if extra:
            by_count(pairs, rule, lambda n: sent(kind + 1, ref.at[pl.ds(0, extra), 0, pl.ds(0, n)]))

    sent_lines(0, ends(near), any_end, red)
    sent_lines(2, ends(range(NEAR, zs - 1)), any_through, red)
    sent(4, red.at[:, 0, 0])
    sent(5, red.at[pl.ds(0, plain), 0, pl.ds(0, zs - 1)])
    sent(6, xb.at[:, 0])
    sent(7, packed.at[:, 0])
    sent(8, red.at[pl.ds(0, plain), 0])
    sent_lines(10, ends(near), any_end, red)
    sent_lines(12, ends(far), any_end, red)
    if extra:
        sent(9, got_y.at[pl.ds(0, extra), 0])
    spot = rb.at[0, 0, pl.ds(0, zs - 1)]
    send(spot, spot, route_s.at[0], route_r.at[0], core_dev).wait_send()
    route_side(side).wait_send()
    route_core(core).wait_send()


def local(wide, interpret, tokens, expert_ids, gates, w_gate, w_up, w_down):
    rows, model = tokens.shape
    hidden = w_gate.shape[2]
    batches = BATCHES if rows % BATCHES == 0 else 1
    part = rows // batches
    fold = 16 // math.gcd(16, part)
    span = fold * CHUNK
    chunks = model // span
    total = batches * chunks
    split = min(SPLIT, chunks)
    extra = batches * split
    zs = wide // (CORES * SIDES)
    pad_rows = -(-rows // 16) * 16
    unit = part * fold
    size = fold * unit
    lines = wide * part
    slots = 2 * min(NEAR, zs - 1)

    any_space = pl.BlockSpec(memory_space=pl.ANY)
    dma = pltpu.SemaphoreType.DMA
    out = pl.pallas_call(
        functools.partial(kernel, wide, rows, batches, fold, split),
        out_shape=jax.ShapeDtypeStruct((rows, model), BF16),
        in_specs=[any_space] + [pl.BlockSpec(memory_space=pltpu.VMEM)] * 2 + [any_space] * 3,
        out_specs=pl.BlockSpec(memory_space=pltpu.VMEM),
        scratch_shapes=[
            pltpu.VMEM((rows, model), BF16),
            pltpu.VMEM((pad_rows, model), BF16),
            pltpu.VMEM((pad_rows, LANES), BF16),
            pltpu.VMEM((total, CORES, SIDES, zs, unit, CHUNK), BF16),
            pltpu.VMEM((CORES, SIDES, zs, pad_rows, LANES), BF16),
            pltpu.VMEM((chunks, 2 * EXP_G, span, hidden), BF16),
            pltpu.VMEM((chunks, EXP_G * hidden, span), BF16),
            pltpu.VMEM((2 * EXP_G, lines, hidden), F32),
            pltpu.VMEM((batches, lines, EXP_G * hidden), BF16),
            pltpu.VMEM((size, size), BF16),
            pltpu.VMEM((size, size), BF16),
            pltpu.VMEM((total, CORES, SIDES, zs, unit, CHUNK), BF16),
            pltpu.VMEM((total, SIDES, zs, unit, CHUNK), BF16),
            pltpu.VMEM((total, SIDES, zs, unit, CHUNK), BF16),
            pltpu.VMEM((total, zs, unit, CHUNK), BF16),
            pltpu.VMEM((total, SIDES, slots, unit, CHUNK), BF16),
            pltpu.VMEM((total if zs - 1 > NEAR else 1, SIDES, zs, unit, CHUNK), BF16),
            pltpu.VMEM((total if split else 1, 2, unit, CHUNK), BF16),
            pltpu.VMEM((chunks, batches * unit, CHUNK), BF16),
            dma(()),
            dma(()),
            dma((chunks,)),
            dma((chunks,)),
            dma((3,)),
            dma((zs + 2,)),
            dma((14,)),
            dma((total + extra, slots)),
            dma((total + extra, zs - 1 - NEAR) if zs - 1 > NEAR else (1, 1)),
            dma((total,)),
            dma((total,)),
            dma((total,)),
            dma((total,)),
            dma((total + extra,)),
            dma((total + extra, zs - 1 - NEAR) if zs - 1 > NEAR else (1, 1)),
        ],
        compiler_params=pltpu.CompilerParams(collective_id=0, has_side_effects=True, vmem_limit_bytes=67043328),
        **interpret,
    )(tokens, expert_ids.T, gates.T, w_gate, w_up, w_down)
    return out


def solution(mesh, interpret=None):
    return jax.shard_map(
        functools.partial(local, mesh.shape["wide"], interpret or {}),
        mesh=mesh,
        in_specs=(
            P(("parts", "wide"), None),
            P(("parts", "wide"), None),
            P(("parts", "wide"), None),
            P(None, None, "wide"),
            P(None, None, "wide"),
            P(None, "wide", None),
        ),
        out_specs=P(("parts", "wide"), None),
        check_vma=False,
    )
```

```python
import functools
import math

import jax
import jax.numpy as jnp
from jax import lax
from jax.experimental import pallas as pl
from jax.experimental.pallas import tpu as pltpu
from jax.sharding import PartitionSpec as P

GROUPS = 8
EXP_G = 2
CORES = 2
SIDES = 2
LANES = 128
CHUNK = 256
BATCHES = 1
SPLIT = 0
AHEAD = 20
SPLIT_AHEAD = 0
LAG_RELAY = 2
LAG_SIDE = 4
LAG_USE = 5
LAG_SUM = 2
LAG_Z = 4
LAG_ZR = 6
LAG_END = 10
NEAR = 2
F32 = jnp.float32
BF16 = jnp.bfloat16


def floor_div(value, by):
    return jnp.floor((value + 0.5) * (1.0 / by))


def iota_f32(shape, dim):
    return lax.broadcasted_iota(jnp.int32, shape, dim).astype(F32)


def one_hot(match):
    return match.astype(F32).astype(BF16)


def kernel(
    wide, rows, batches, fold, split,
    tok_ref, ids_ref, gate_ref, wg_ref, wu_ref, wd_ref, out_ref,
    tok, padded, r_ref, xb, rb, wb, wdb, acc, hid, perm, perm_back, packed, got_core, red, got_side, got_z, relay, got_y, fin,
    tok_sem, own_sem, w_sem, d_sem, route_s, route_r, out_s, az_r, af_r, ay_r, ac_r, bc_r, by_r, bo_r, bz_r, br_r,
):
    zs = wide // (CORES * SIDES)
    total = xb.shape[0]
    chunks = total // batches
    hidden = wg_ref.shape[2]
    part = rows // batches
    unit = part * fold
    span = fold * CHUNK
    units = wide
    groups = units // fold
    size = fold * unit
    lines = units * part
    pad_rows = r_ref.shape[0]
    near = range(1, min(NEAR, zs - 1) + 1)
    far = range(NEAR + 1, zs)
    extra = batches * split

    me = lax.axis_index("wide")
    core = lax.rem(me, CORES)
    chip = me // CORES
    side = lax.rem(chip, SIDES)
    z = chip // SIDES
    other_core = 1 - core
    other_side = 1 - side
    halves = (side, other_side)

    def at(z_at, side_at, core_at):
        return {"wide": (z_at * SIDES + side_at) * CORES + core_at}

    core_dev = at(z, side, other_core)
    side_dev = at(z, other_side, core)

    def inside(value):
        return (value >= 0) & (value < zs)

    def around(distances):
        return [(d, sign, z + sign * d, (d - 1) * 2 + (sign + 1) // 2) for d in distances for sign in (-1, 1)]

    def send(src, dst, s_sem, r_sem, dev):
        return pltpu.make_async_remote_copy(
            src_ref=src, dst_ref=dst, send_sem=s_sem, recv_sem=r_sem, device_id=dev, device_id_type=pl.DeviceIdType.MESH
        )

    def up_copies(k):
        rows_of = pl.ds(pl.multiple_of(k * span, span), span)
        return [
            pltpu.make_async_copy(wg_ref.at[:, rows_of, :], wb.at[k, pl.ds(0, EXP_G)], w_sem.at[k]),
            pltpu.make_async_copy(wu_ref.at[:, rows_of, :], wb.at[k, pl.ds(EXP_G, EXP_G)], w_sem.at[k]),
        ]

    def up_wait(k):
        pltpu.make_async_copy(wb.at[k], wb.at[k], w_sem.at[k]).wait()

    def down_copies(k):
        columns = pl.ds(pl.multiple_of(k * span, span), span)
        return [
            pltpu.make_async_copy(wd_ref.at[e, :, columns], wdb.at[k, pl.ds(e * hidden, hidden), :], d_sem.at[k])
            for e in range(EXP_G)
        ]

    def down_wait(k):
        pltpu.make_async_copy(wdb.at[k], wdb.at[k], d_sem.at[k]).wait()

    def line_of(q, rel, first):
        return q if rel == 0 else total + q // chunks * split + lax.rem(q, chunks) - first

    def by_count(pairs, rule, act):
        here = sum(rule(z + sign * d, z - sign).astype(jnp.int32) for d, sign in pairs)
        held_here = {sum(bool(rule(spot + sign * d, spot - sign)) for d, sign in pairs) for spot in range(zs)}
        for n in sorted(held_here - {0}):
            @pl.when(here == n)
            def _():
                act(n)

    def ends(distances):
        return [(d, sign) for d in distances for sign in (-1, 1)]

    def any_end(value, behind):
        return inside(value)

    def any_through(value, behind):
        return inside(value) & inside(behind)

    def any_first(value, behind):
        return inside(value) & ((behind < 0) | (behind >= zs))

    def z_hop(q, rel, src, dst, kind, r_sem):
        spot = xb.at[q, core, halves[rel], src]
        return send(spot, spot, out_s.at[kind], r_sem, at(dst, side, core))

    def y_hop(q, half, src, kind):
        spot = xb.at[q, core, half, src]
        return send(spot, spot, out_s.at[kind], ay_r.at[q], side_dev)

    def core_hop(q, owner, rel):
        spot = xb.at[q, owner, halves[rel]]
        return send(spot, spot, out_s.at[6], ac_r.at[q], core_dev)

    def z_own(q, rel):
        line = line_of(q, rel, chunks - split)
        for d, sign, dst, slot in reversed(around(near)):
            @pl.when(inside(dst))
            def _():
                z_hop(q, rel, z, dst, rel, az_r.at[line, slot]).start()

    def z_onward(q, rel, distances, onward):
        for d, sign, src, slot in around(distances):
            @pl.when(inside(src))
            def _():
                if d >= NEAR and d + 1 < zs:
                    @pl.when(inside(z - sign))
                    def _():
                        z_hop(q, rel, src, z - sign, 2 + rel, af_r.at[line_of(q, rel, chunks - split), d - NEAR]).start()
                if onward:
                    y_hop(q, side, src, 5).start()

    def z_wait(q, rel, distances, r_sem):
        def wait(n):
            spot = xb.at[q, core, halves[rel], pl.ds(0, n)]
            send(spot, spot, out_s.at[0], r_sem, core_dev).wait_recv()

        by_count(ends(distances), any_end, wait)

    def arrive_near(q, rel, onward):
        line = line_of(q, rel, chunks - split)
        for d, sign, src, slot in around(near):
            @pl.when(inside(z - sign * d))
            def _():
                z_hop(q, rel, z - sign * d, z - sign * d, 0, az_r.at[line, slot]).wait_recv()
                if d >= NEAR and d + 1 < zs:
                    @pl.when(inside(z + sign))
                    def _():
                        z_hop(q, rel, z - sign * d, z + sign, 2 + rel, af_r.at[line, d - NEAR]).start()
                if onward:
                    y_hop(q, side, z - sign * d, 5).start()

    def arrive_far(q, rel, onward):
        for d in far:
            z_wait(q, rel, [d], af_r.at[line_of(q, rel, chunks - split), d - NEAR - 1])
            z_onward(q, rel, [d], onward)

    def route_z(step):
        dst = lax.rem(z + step, zs)
        return send(r_ref, rb.at[core, side, z], route_s.at[0], route_r.at[step], at(dst, side, core))

    def route_side(half):
        return send(rb.at[core, half], rb.at[core, half], route_s.at[1], route_r.at[zs], side_dev)

    def route_core(owner):
        return send(rb.at[owner], rb.at[owner], route_s.at[2], route_r.at[zs + 1], core_dev)

    def route_local():
        return pltpu.make_async_copy(r_ref, rb.at[core, side, z], own_sem)

    def back_core(p):
        return send(packed.at[p, other_core], got_core.at[p], out_s.at[7], bc_r.at[p], core_dev)

    def back_side(p, dst):
        return send(red.at[p, 1, dst], got_side.at[p, dst], out_s.at[8], by_r.at[p], side_dev)

    def back_own(p):
        return send(red.at[p, 1, z], got_side.at[p, z], out_s.at[14], bo_r.at[p], side_dev)

    def back_last(p):
        return send(got_y.at[p, 0], got_y.at[p, 1], out_s.at[9], by_r.at[p], side_dev)

    def back_z(p, rel, dst, slot):
        r_sem = bz_r.at[line_of(p, rel, 0)]
        return send(red.at[p, rel, dst], got_z.at[p, rel, slot], out_s.at[10 + rel], r_sem, at(dst, side, core))

    def back_relay(p, rel, d, dst, to):
        r_sem = br_r.at[line_of(p, rel, 0), d]
        return send(red.at[p, rel, dst], relay.at[p, rel, dst], out_s.at[12 + rel], r_sem, at(to, side, core))

    def reduce_out(p, rel, d, sign, dst, slot):
        if d <= NEAR:
            back_z(p, rel, dst, slot).start()
        else:
            back_relay(p, rel, d - NEAR - 1, dst, z + sign).start()

    def reduce_first(p, rel):
        for d, sign, dst, slot in reversed(around(range(1, zs))):
            ready = inside(dst) if d < NEAR else any_first(dst, z - sign)

            @pl.when(ready)
            def _():
                reduce_out(p, rel, d, sign, dst, slot)

    def reduce_second(p, rel):
        for d in reversed(range(NEAR, zs - 1)):
            def wait(n):
                spot = relay.at[p, rel, pl.ds(0, n)]
                send(spot, spot, out_s.at[0], br_r.at[line_of(p, rel, 0), d - NEAR], core_dev).wait_recv()

            by_count(ends([d]), any_through, wait)
            for _, sign, dst, slot in around([d]):
                @pl.when(any_through(dst, z - sign))
                def _():
                    red[p, rel, dst] = (red[p, rel, dst].astype(F32) + relay[p, rel, dst].astype(F32)).astype(BF16)
                    reduce_out(p, rel, d, sign, dst, slot)

    def reduce_last(p, rel):
        def wait(n):
            spot = got_z.at[p, rel, pl.ds(0, n)]
            send(spot, spot, out_s.at[0], bz_r.at[line_of(p, rel, 0)], core_dev).wait_recv()

        by_count(ends(near), any_end, wait)
        done = red[p, rel, z].astype(F32)
        for d, sign, src, slot in around(near):
            done = done + got_z[p, rel, slot].astype(F32)
        return done

    token_copy = pltpu.make_async_copy(tok_ref, tok, tok_sem)
    token_copy.start()
    for copy in up_copies(0):
        copy.start()

    for d, sign, src, slot in around(near):
        @pl.when(jnp.logical_not(inside(z - sign * d)))
        def _():
            @pl.loop(0, total)
            def _(p):
                for rel in range(SIDES):
                    got_z[p, rel, slot] = jnp.zeros((unit, CHUNK), BF16)

    barrier = pltpu.get_barrier_semaphore()
    for step in range(1, zs):
        pl.semaphore_signal(barrier, inc=1, device_id=at(lax.rem(z + step, zs), side, core), device_id_type=pl.DeviceIdType.MESH)
    pl.semaphore_signal(barrier, inc=1, device_id=side_dev, device_id_type=pl.DeviceIdType.MESH)
    pl.semaphore_signal(barrier, inc=1, device_id=core_dev, device_id_type=pl.DeviceIdType.MESH)

    def place(index):
        batch = floor_div(index, unit)
        rest = index - batch * unit
        block = floor_div(rest, part)
        return block * pad_rows + batch * part + rest - block * part

    held = batches * unit
    into = one_hot(iota_f32((held, fold * pad_rows), 1) == place(iota_f32((held, 1), 0)))
    spread = one_hot(iota_f32((pad_rows, rows), 0) == iota_f32((pad_rows, rows), 1))
    token_copy.wait()
    padded[...] = jnp.dot(spread, tok[...], preferred_element_type=F32).astype(BF16)

    def pack(k):
        tiles = jnp.concatenate([padded[:, k * span + f * CHUNK:k * span + (f + 1) * CHUNK] for f in range(fold)], axis=0)
        mine = jnp.dot(into, tiles, preferred_element_type=F32).astype(BF16)
        for b in range(batches):
            xb[b * chunks + k, core, side, z] = mine[b * unit:(b + 1) * unit]

    def offer(q):
        y_hop(q, side, z, 4).start()
        z_own(q, 0)

    token = lax.broadcasted_iota(jnp.int32, (LANES, rows), 0)
    route = jnp.zeros((LANES, rows), F32)
    for slot in range(ids_ref.shape[0]):
        route = route + jnp.where(ids_ref[slot:slot + 1, :] == token, gate_ref[slot:slot + 1, :], 0.0)
    r_ref[...] = lax.dot_general(spread, route.astype(BF16), (((1,), (1,)), ((), ())), preferred_element_type=F32).astype(BF16)
    route_local().start()
    pack(0)
    pl.semaphore_wait(barrier, zs + 1)
    offer(0)
    for step in range(1, zs):
        route_z(step).start()
    for k in range(1, chunks):
        pack(k)
        if k < AHEAD:
            offer(k)
    for q in range(chunks, min(AHEAD, total)):
        offer(q)

    def order(index):
        first = floor_div(index, unit)
        rest = index - first * unit
        second = floor_div(rest, part)
        return second * unit + first * part + (rest - second * part)

    perm[...] = one_hot(order(iota_f32((size, 1), 0)) == iota_f32((size, size), 1))
    perm_back[...] = one_hot(iota_f32((size, size), 0) == order(iota_f32((1, size), 1)))
    acc[...] = jnp.zeros_like(acc)

    lag_down = LAG_USE + chunks - 1

    def staged(lag, count=total):
        def wrap(body):
            def run(now):
                @pl.when((now >= lag) & (now < count + lag))
                def _():
                    body(now - lag)
            return run
        return wrap

    def either(test, yes, no):
        if split == 0:
            no()
        else:
            pl.when(test)(yes)
            pl.when(jnp.logical_not(test))(no)

    def gather_split(q):
        return lax.rem(q, chunks) >= chunks - split

    def scatter_split(p):
        return lax.rem(p, chunks) < split

    @staged(-AHEAD)
    def stage_offer(q):
        offer(q)

    @staged(0, chunks)
    def stage_weights(k):
        @pl.when(k + 1 < chunks)
        def _():
            for copy in up_copies(k + 1):
                copy.start()

        for copy in down_copies(k):
            copy.start()

    @staged(0)
    def stage_arrive(q):
        def both():
            arrive_near(q, 0, False)
            arrive_near(q, 1, False)

        either(gather_split(q), both, lambda: arrive_near(q, 0, True))

        @pl.when(q == chunks // 2)
        def _():
            route_local().wait()
            for step in range(1, zs):
                route_z(step).wait_recv()
            route_side(side).start()

    @staged(-SPLIT_AHEAD)
    def stage_split(q):
        def both():
            y_hop(q, other_side, z, 4).wait_recv()
            z_own(q, 1)

        either(gather_split(q), both, lambda: None)

    @staged(LAG_RELAY)
    def stage_relay(q):
        def both():
            arrive_far(q, 0, False)
            arrive_far(q, 1, False)
            core_hop(q, core, 0).start()
            core_hop(q, core, 1).start()

        def one():
            arrive_far(q, 0, True)
            core_hop(q, core, 0).start()

        either(gather_split(q), both, one)

    @staged(LAG_SIDE)
    def stage_side(q):
        def one():
            spot = xb.at[q, core, other_side]
            send(spot, spot, out_s.at[5], ay_r.at[q], side_dev).wait_recv()
            core_hop(q, core, 1).start()

        either(gather_split(q), lambda: None, one)

        @pl.when(q == chunks // 2)
        def _():
            route_side(other_side).wait_recv()
            route_core(core).start()

    @staged(LAG_USE)
    def stage_up(q):
        spot = xb.at[q, other_core]
        send(spot, spot, out_s.at[6], ac_r.at[q], core_dev).wait_recv()
        k = lax.rem(q, chunks)

        @pl.when(q < chunks)
        def _():
            up_wait(k)

        folded = xb[q].reshape(groups, size, CHUNK)
        moved = jnp.dot(perm[...], jnp.concatenate([folded[g] for g in range(groups)], axis=1), preferred_element_type=F32).astype(BF16)
        left = jnp.concatenate([
            jnp.concatenate([moved[f * unit:(f + 1) * unit, g * CHUNK:(g + 1) * CHUNK] for f in range(fold)], axis=1)
            for g in range(groups)
        ], axis=0)
        for e in range(EXP_G):
            acc[2 * e] += jnp.dot(left, wb[k, e], preferred_element_type=F32)
            acc[2 * e + 1] += jnp.dot(left, wb[k, EXP_G + e], preferred_element_type=F32)

        @pl.when(k == chunks - 1)
        def _():
            b = q // chunks

            @pl.when(b == 0)
            def _():
                route_core(other_core).wait_recv()

            line = iota_f32((1, units * pad_rows), 1)
            unit_of = floor_div(line, pad_rows)
            row_of = line - unit_of * pad_rows - (b * part).astype(F32)
            wanted = jnp.where((row_of >= 0) & (row_of < part), unit_of * part + row_of, -1.0)
            pick = one_hot(iota_f32((lines, units * pad_rows), 0) == wanted)
            scales = jnp.dot(pick, rb[...].reshape(units * pad_rows, LANES), preferred_element_type=F32)
            lane = lax.broadcasted_iota(jnp.int32, (lines, LANES), 1)
            first_expert = me // (wide // GROUPS) * EXP_G
            for e in range(EXP_G):
                scale = jnp.sum(jnp.where(lane == first_expert + e, scales, 0.0), axis=1, keepdims=True)
                gate = acc[2 * e]
                value = gate / (1.0 + jnp.exp(-gate)) * acc[2 * e + 1]
                hid[b, :, e * hidden:(e + 1) * hidden] = (value * scale).astype(BF16)
            acc[...] = jnp.zeros_like(acc)

    @staged(lag_down)
    def stage_down(p):
        k = lax.rem(p, chunks)

        @pl.when(p < chunks)
        def _():
            down_wait(k)

        down = jnp.dot(hid[p // chunks], wdb[k], preferred_element_type=F32).astype(BF16)
        stacked = jnp.concatenate([
            jnp.concatenate([down[g * unit:(g + 1) * unit, f * CHUNK:(f + 1) * CHUNK] for f in range(fold)], axis=0)
            for g in range(groups)
        ], axis=1)
        moved = jnp.dot(perm_back[...], stacked, preferred_element_type=F32).astype(BF16)
        flat = jnp.concatenate([moved[:, g * CHUNK:(g + 1) * CHUNK] for g in range(groups)], axis=0)
        packed[p] = flat.reshape(CORES, SIDES, zs, unit, CHUNK)
        back_core(p).start()

    @staged(lag_down + LAG_SUM)
    def stage_sum(p):
        back_core(p).wait_recv()
        for rel in (1, 0):
            red[p, rel] = (packed[p, core, halves[rel]].astype(F32) + got_core[p, halves[rel]].astype(F32)).astype(BF16)

        def both():
            reduce_first(p, 0)
            reduce_first(p, 1)

        def one():
            for d, sign, dst, slot in reversed(around(range(1, zs))):
                @pl.when(inside(dst))
                def _():
                    back_side(p, dst).start()

        either(scatter_split(p), both, one)

        @pl.when(p == total - 1)
        def _():
            @pl.loop(0, total)
            def _(j):
                either(scatter_split(j), lambda: None, lambda: back_own(j).start())

    @staged(lag_down + LAG_Z)
    def stage_z(p):
        def both():
            reduce_second(p, 0)
            reduce_second(p, 1)

        def one():
            spot = got_side.at[p, pl.ds(0, zs - 1)]
            send(spot, spot, out_s.at[8], by_r.at[p], side_dev).wait_recv()
            for step in range(1, zs):
                dst = lax.rem(z + step, zs)
                red[p, 0, dst] = (red[p, 0, dst].astype(F32) + got_side[p, dst].astype(F32)).astype(BF16)
            reduce_first(p, 0)

        either(scatter_split(p), both, one)

    @staged(lag_down + LAG_ZR)
    def stage_zr(p):
        def both():
            got_y[p, 0] = reduce_last(p, 1).astype(BF16)
            back_last(p).start()

        either(scatter_split(p), both, lambda: reduce_second(p, 0))

    @staged(lag_down + LAG_END)
    def stage_end(p):
        b = p // chunks
        k = lax.rem(p, chunks)
        spot = pl.ds(pl.multiple_of(b * unit, unit), unit)

        def both():
            back_last(p).wait_recv()
            fin[k, spot] = (reduce_last(p, 0) + got_y[p, 1].astype(F32)).astype(BF16)

        def one():
            back_own(p).wait_recv()
            fin[k, spot] = (reduce_last(p, 0) + got_side[p, z].astype(F32)).astype(BF16)

        either(scatter_split(p), both, one)

        @pl.when(b == batches - 1)
        def _():
            out_of = one_hot(iota_f32((fold * pad_rows, held), 0) == place(iota_f32((1, held), 1)))
            flat = jnp.dot(out_of, fin[k], preferred_element_type=F32).astype(BF16)
            for f in range(fold):
                columns = pl.ds(pl.multiple_of(k * span + f * CHUNK, CHUNK), CHUNK)
                out_ref[:, columns] = flat[f * pad_rows:f * pad_rows + rows]

    @pl.loop(0, total + lag_down + LAG_END)
    def _(now):
        stage_weights(now)
        stage_offer(now)
        stage_arrive(now)
        stage_split(now)
        stage_relay(now)
        stage_side(now)
        stage_sum(now)
        stage_z(now)
        stage_zr(now)
        stage_end(now)
        stage_up(now)
        stage_down(now)

    def sent(kind, spot):
        send(spot, spot, out_s.at[kind], ay_r.at[0], core_dev).wait_send()

    plain = total - extra

    def sent_lines(kind, pairs, rule, ref):
        by_count(pairs, rule, lambda n: sent(kind, ref.at[:, 0, pl.ds(0, n)]))
        if extra:
            by_count(pairs, rule, lambda n: sent(kind + 1, ref.at[pl.ds(0, extra), 0, pl.ds(0, n)]))

    sent_lines(0, ends(near), any_end, red)
    sent_lines(2, ends(range(NEAR, zs - 1)), any_through, red)
    sent(4, red.at[:, 0, 0])
    sent(5, red.at[pl.ds(0, plain), 0, pl.ds(0, zs - 1)])
    sent(6, xb.at[:, 0])
    sent(7, packed.at[:, 0])
    sent(8, red.at[pl.ds(0, plain), 0, pl.ds(0, zs - 1)])
    sent(14, red.at[pl.ds(0, plain), 0, 0])
    sent_lines(10, ends(near), any_end, red)
    sent_lines(12, ends(far), any_end, red)
    if extra:
        sent(9, got_y.at[pl.ds(0, extra), 0])
    spot = rb.at[0, 0, pl.ds(0, zs - 1)]
    send(spot, spot, route_s.at[0], route_r.at[0], core_dev).wait_send()
    route_side(side).wait_send()
    route_core(core).wait_send()


def local(wide, interpret, tokens, expert_ids, gates, w_gate, w_up, w_down):
    rows, model = tokens.shape
    hidden = w_gate.shape[2]
    batches = BATCHES if rows % BATCHES == 0 else 1
    part = rows // batches
    fold = 16 // math.gcd(16, part)
    span = fold * CHUNK
    chunks = model // span
    total = batches * chunks
    split = min(SPLIT, chunks)
    extra = batches * split
    zs = wide // (CORES * SIDES)
    pad_rows = -(-rows // 16) * 16
    unit = part * fold
    size = fold * unit
    lines = wide * part
    slots = 2 * min(NEAR, zs - 1)

    any_space = pl.BlockSpec(memory_space=pl.ANY)
    dma = pltpu.SemaphoreType.DMA
    out = pl.pallas_call(
        functools.partial(kernel, wide, rows, batches, fold, split),
        out_shape=jax.ShapeDtypeStruct((rows, model), BF16),
        in_specs=[any_space] + [pl.BlockSpec(memory_space=pltpu.VMEM)] * 2 + [any_space] * 3,
        out_specs=pl.BlockSpec(memory_space=pltpu.VMEM),
        scratch_shapes=[
            pltpu.VMEM((rows, model), BF16),
            pltpu.VMEM((pad_rows, model), BF16),
            pltpu.VMEM((pad_rows, LANES), BF16),
            pltpu.VMEM((total, CORES, SIDES, zs, unit, CHUNK), BF16),
            pltpu.VMEM((CORES, SIDES, zs, pad_rows, LANES), BF16),
            pltpu.VMEM((chunks, 2 * EXP_G, span, hidden), BF16),
            pltpu.VMEM((chunks, EXP_G * hidden, span), BF16),
            pltpu.VMEM((2 * EXP_G, lines, hidden), F32),
            pltpu.VMEM((batches, lines, EXP_G * hidden), BF16),
            pltpu.VMEM((size, size), BF16),
            pltpu.VMEM((size, size), BF16),
            pltpu.VMEM((total, CORES, SIDES, zs, unit, CHUNK), BF16),
            pltpu.VMEM((total, SIDES, zs, unit, CHUNK), BF16),
            pltpu.VMEM((total, SIDES, zs, unit, CHUNK), BF16),
            pltpu.VMEM((total, zs, unit, CHUNK), BF16),
            pltpu.VMEM((total, SIDES, slots, unit, CHUNK), BF16),
            pltpu.VMEM((total if zs - 1 > NEAR else 1, SIDES, zs, unit, CHUNK), BF16),
            pltpu.VMEM((total if split else 1, 2, unit, CHUNK), BF16),
            pltpu.VMEM((chunks, batches * unit, CHUNK), BF16),
            dma(()),
            dma(()),
            dma((chunks,)),
            dma((chunks,)),
            dma((3,)),
            dma((zs + 2,)),
            dma((15,)),
            dma((total + extra, slots)),
            dma((total + extra, zs - 1 - NEAR) if zs - 1 > NEAR else (1, 1)),
            dma((total,)),
            dma((total,)),
            dma((total,)),
            dma((total,)),
            dma((total,)),
            dma((total + extra,)),
            dma((total + extra, zs - 1 - NEAR) if zs - 1 > NEAR else (1, 1)),
        ],
        compiler_params=pltpu.CompilerParams(collective_id=0, has_side_effects=True, vmem_limit_bytes=67043328),
        **interpret,
    )(tokens, expert_ids.T, gates.T, w_gate, w_up, w_down)
    return out


def solution(mesh, interpret=None):
    return jax.shard_map(
        functools.partial(local, mesh.shape["wide"], interpret or {}),
        mesh=mesh,
        in_specs=(
            P(("parts", "wide"), None),
            P(("parts", "wide"), None),
            P(("parts", "wide"), None),
            P(None, None, "wide"),
            P(None, None, "wide"),
            P(None, "wide", None),
        ),
        out_specs=P(("parts", "wide"), None),
        check_vma=False,
    )
```

```python
import functools
import math

import jax
import jax.numpy as jnp
from jax import lax
from jax.experimental import pallas as pl
from jax.experimental.pallas import tpu as pltpu
from jax.sharding import PartitionSpec as P

GROUPS = 8
EXP_G = 2
CORES = 2
SIDES = 2
LANES = 128
CHUNK = 256
BATCHES = 1
SPLIT_IN = 1
SPLIT_OUT = 0
AHEAD = 20
SPLIT_AHEAD = 4
LAG_RELAY = 2
LAG_SIDE = 4
LAG_USE = 5
LAG_SUM = 2
LAG_Z = 4
LAG_ZR = 6
LAG_END = 10
NEAR = 2
F32 = jnp.float32
BF16 = jnp.bfloat16


def floor_div(value, by):
    return jnp.floor((value + 0.5) * (1.0 / by))


def iota_f32(shape, dim):
    return lax.broadcasted_iota(jnp.int32, shape, dim).astype(F32)


def one_hot(match):
    return match.astype(F32).astype(BF16)


def kernel(
    wide, rows, batches, fold, split_in, split_out,
    tok_ref, ids_ref, gate_ref, wg_ref, wu_ref, wd_ref, out_ref,
    tok, r_ref, xb, rb, wb, wdb, acc, hid, perm, perm_back, packed, got_core, red, got_side, got_z, relay, got_y, fin, scale_ref, out_v,
    tok_sem, own_sem, w_sem, d_sem, route_s, route_r, out_s, az_r, af_r, ay_r, ac_r, bc_r, by_r, bo_r, bz_r, br_r,
):
    zs = wide // (CORES * SIDES)
    total = xb.shape[0]
    chunks = total // batches
    hidden = wg_ref.shape[2]
    part = rows // batches
    unit = part * fold
    span = fold * CHUNK
    units = wide
    groups = units // fold
    size = fold * unit
    lines = units * part
    pad_rows = r_ref.shape[0]
    near = range(1, min(NEAR, zs - 1) + 1)
    far = range(NEAR + 1, zs)
    extra_in = batches * split_in
    extra_out = batches * split_out

    me = lax.axis_index("wide")
    core = lax.rem(me, CORES)
    chip = me // CORES
    side = lax.rem(chip, SIDES)
    z = chip // SIDES
    other_core = 1 - core
    other_side = 1 - side
    halves = (side, other_side)

    def at(z_at, side_at, core_at):
        return {"wide": (z_at * SIDES + side_at) * CORES + core_at}

    core_dev = at(z, side, other_core)
    side_dev = at(z, other_side, core)

    def inside(value):
        return (value >= 0) & (value < zs)

    def around(distances):
        return [(d, sign, z + sign * d, (d - 1) * 2 + (sign + 1) // 2) for d in distances for sign in (-1, 1)]

    def send(src, dst, s_sem, r_sem, dev):
        return pltpu.make_async_remote_copy(
            src_ref=src, dst_ref=dst, send_sem=s_sem, recv_sem=r_sem, device_id=dev, device_id_type=pl.DeviceIdType.MESH
        )

    def up_copies(k):
        rows_of = pl.ds(pl.multiple_of(k * span, span), span)
        return [
            pltpu.make_async_copy(wg_ref.at[:, rows_of, :], wb.at[k, pl.ds(0, EXP_G)], w_sem.at[k]),
            pltpu.make_async_copy(wu_ref.at[:, rows_of, :], wb.at[k, pl.ds(EXP_G, EXP_G)], w_sem.at[k]),
        ]

    def up_wait(k):
        pltpu.make_async_copy(wb.at[k], wb.at[k], w_sem.at[k]).wait()

    def down_copies(k):
        columns = pl.ds(pl.multiple_of(k * span, span), span)
        return [
            pltpu.make_async_copy(wd_ref.at[e, :, columns], wdb.at[k, pl.ds(e * hidden, hidden), :], d_sem.at[k])
            for e in range(EXP_G)
        ]

    def down_wait(k):
        pltpu.make_async_copy(wdb.at[k], wdb.at[k], d_sem.at[k]).wait()

    def line_in(q, rel):
        return q if rel == 0 else total + q // chunks * split_in + lax.rem(q, chunks) - (chunks - split_in)

    def line_out(p, rel):
        return p if rel == 0 else total + p // chunks * split_out + lax.rem(p, chunks)

    def by_count(pairs, rule, act):
        here = sum(rule(z + sign * d, z - sign).astype(jnp.int32) for d, sign in pairs)
        held_here = {sum(bool(rule(spot + sign * d, spot - sign)) for d, sign in pairs) for spot in range(zs)}
        for n in sorted(held_here - {0}):
            @pl.when(here == n)
            def _():
                act(n)

    def ends(distances):
        return [(d, sign) for d in distances for sign in (-1, 1)]

    def any_end(value, behind):
        return inside(value)

    def any_through(value, behind):
        return inside(value) & inside(behind)

    def any_first(value, behind):
        return inside(value) & ((behind < 0) | (behind >= zs))

    def z_hop(q, rel, src, dst, kind, r_sem):
        spot = xb.at[q, core, halves[rel], src]
        return send(spot, spot, out_s.at[kind], r_sem, at(dst, side, core))

    def y_hop(q, half, src, kind):
        spot = xb.at[q, core, half, src]
        return send(spot, spot, out_s.at[kind], ay_r.at[q], side_dev)

    def core_hop(q, owner, rel):
        spot = xb.at[q, owner, halves[rel]]
        return send(spot, spot, out_s.at[6], ac_r.at[q], core_dev)

    def z_own(q, rel):
        line = line_in(q, rel)
        for d, sign, dst, slot in reversed(around(near)):
            @pl.when(inside(dst))
            def _():
                z_hop(q, rel, z, dst, rel, az_r.at[line, slot]).start()

    def z_onward(q, rel, distances, onward):
        for d, sign, src, slot in around(distances):
            @pl.when(inside(src))
            def _():
                if d >= NEAR and d + 1 < zs:
                    @pl.when(inside(z - sign))
                    def _():
                        z_hop(q, rel, src, z - sign, 2 + rel, af_r.at[line_in(q, rel), d - NEAR]).start()
                if onward:
                    y_hop(q, side, src, 5).start()

    def z_wait(q, rel, distances, r_sem):
        def wait(n):
            spot = xb.at[q, core, halves[rel], pl.ds(0, n)]
            send(spot, spot, out_s.at[0], r_sem, core_dev).wait_recv()

        by_count(ends(distances), any_end, wait)

    def arrive_near(q, rel, onward):
        line = line_in(q, rel)
        for d, sign, src, slot in around(near):
            @pl.when(inside(z - sign * d))
            def _():
                z_hop(q, rel, z - sign * d, z - sign * d, 0, az_r.at[line, slot]).wait_recv()
                if d >= NEAR and d + 1 < zs:
                    @pl.when(inside(z + sign))
                    def _():
                        z_hop(q, rel, z - sign * d, z + sign, 2 + rel, af_r.at[line, d - NEAR]).start()
                if onward:
                    y_hop(q, side, z - sign * d, 5).start()

    def arrive_far(q, rel, onward):
        for d in far:
            z_wait(q, rel, [d], af_r.at[line_in(q, rel), d - NEAR - 1])
            z_onward(q, rel, [d], onward)

    def route_z(step):
        dst = lax.rem(z + step, zs)
        return send(r_ref, rb.at[core, side, z], route_s.at[0], route_r.at[step], at(dst, side, core))

    def route_side(half):
        return send(rb.at[core, half], rb.at[core, half], route_s.at[1], route_r.at[zs], side_dev)

    def route_core(owner):
        return send(rb.at[owner], rb.at[owner], route_s.at[2], route_r.at[zs + 1], core_dev)

    def route_local():
        return pltpu.make_async_copy(r_ref, rb.at[core, side, z], own_sem)

    def back_core(p):
        return send(packed.at[p, other_core], got_core.at[p], out_s.at[7], bc_r.at[p], core_dev)

    def back_side(p, dst):
        return send(red.at[p, 1, dst], got_side.at[p, dst], out_s.at[8], by_r.at[p], side_dev)

    def back_own(p):
        return send(red.at[p, 1, z], got_side.at[p, z], out_s.at[14], bo_r.at[p], side_dev)

    def back_last(p):
        return send(got_y.at[p, 0], got_y.at[p, 1], out_s.at[9], by_r.at[p], side_dev)

    def back_z(p, rel, dst, slot):
        r_sem = bz_r.at[line_out(p, rel)]
        return send(red.at[p, rel, dst], got_z.at[p, rel, slot], out_s.at[10 + rel], r_sem, at(dst, side, core))

    def back_relay(p, rel, d, dst, to):
        r_sem = br_r.at[line_out(p, rel), d]
        return send(red.at[p, rel, dst], relay.at[p, rel, dst], out_s.at[12 + rel], r_sem, at(to, side, core))

    def reduce_out(p, rel, d, sign, dst, slot):
        if d <= NEAR:
            back_z(p, rel, dst, slot).start()
        else:
            back_relay(p, rel, d - NEAR - 1, dst, z + sign).start()

    def reduce_first(p, rel):
        for d, sign, dst, slot in reversed(around(range(1, zs))):
            ready = inside(dst) if d < NEAR else any_first(dst, z - sign)

            @pl.when(ready)
            def _():
                reduce_out(p, rel, d, sign, dst, slot)

    def reduce_second(p, rel):
        for d in reversed(range(NEAR, zs - 1)):
            def wait(n):
                spot = relay.at[p, rel, pl.ds(0, n)]
                send(spot, spot, out_s.at[0], br_r.at[line_out(p, rel), d - NEAR], core_dev).wait_recv()

            by_count(ends([d]), any_through, wait)
            for _, sign, dst, slot in around([d]):
                @pl.when(any_through(dst, z - sign))
                def _():
                    red[p, rel, dst] = (red[p, rel, dst].astype(F32) + relay[p, rel, dst].astype(F32)).astype(BF16)
                    reduce_out(p, rel, d, sign, dst, slot)

    def reduce_last(p, rel):
        def wait(n):
            spot = got_z.at[p, rel, pl.ds(0, n)]
            send(spot, spot, out_s.at[0], bz_r.at[line_out(p, rel)], core_dev).wait_recv()

        by_count(ends(near), any_end, wait)
        done = red[p, rel, z].astype(F32)
        for d, sign, src, slot in around(near):
            done = done + got_z[p, rel, slot].astype(F32)
        return done

    token_copy = pltpu.make_async_copy(tok_ref, tok, tok_sem)
    token_copy.start()
    for copy in up_copies(0):
        copy.start()

    barrier = pltpu.get_barrier_semaphore()
    for step in range(1, zs):
        pl.semaphore_signal(barrier, inc=1, device_id=at(lax.rem(z + step, zs), side, core), device_id_type=pl.DeviceIdType.MESH)
    pl.semaphore_signal(barrier, inc=1, device_id=side_dev, device_id_type=pl.DeviceIdType.MESH)
    pl.semaphore_signal(barrier, inc=1, device_id=core_dev, device_id_type=pl.DeviceIdType.MESH)

    def place(index):
        batch = floor_div(index, unit)
        rest = index - batch * unit
        block = floor_div(rest, part)
        return block * pad_rows + batch * part + rest - block * part

    held = batches * unit
    into = one_hot(iota_f32((held, fold * pad_rows), 1) == place(iota_f32((held, 1), 0)))
    spread = one_hot(iota_f32((pad_rows, rows), 0) == iota_f32((pad_rows, rows), 1))
    token = lax.broadcasted_iota(jnp.int32, (LANES, rows), 0)
    route = jnp.zeros((LANES, rows), F32)
    for slot in range(ids_ref.shape[0]):
        route = route + jnp.where(ids_ref[slot:slot + 1, :] == token, gate_ref[slot:slot + 1, :], 0.0)
    r_ref[...] = lax.dot_general(spread, route.astype(BF16), (((1,), (1,)), ((), ())), preferred_element_type=F32).astype(BF16)
    route_local().start()
    token_copy.wait()

    def pack(k):
        padded = jnp.dot(spread, tok[:, k * span:(k + 1) * span], preferred_element_type=F32).astype(BF16)
        tiles = jnp.concatenate([padded[:, f * CHUNK:(f + 1) * CHUNK] for f in range(fold)], axis=0)
        mine = jnp.dot(into, tiles, preferred_element_type=F32).astype(BF16)
        for b in range(batches):
            xb[b * chunks + k, core, side, z] = mine[b * unit:(b + 1) * unit]

    def offer(q):
        y_hop(q, side, z, 4).start()
        z_own(q, 0)

    pack(0)
    pl.semaphore_wait(barrier, zs + 1)
    offer(0)
    for step in range(1, zs):
        route_z(step).start()
    for k in range(1, chunks):
        pack(k)
        if k < AHEAD:
            offer(k)
    for q in range(chunks, min(AHEAD, total)):
        offer(q)

    for d, sign, src, slot in around(near):
        @pl.when(jnp.logical_not(inside(z - sign * d)))
        def _():
            @pl.loop(0, total)
            def _(p):
                for rel in range(SIDES if split_out else 1):
                    got_z[p, rel, slot] = jnp.zeros((unit, CHUNK), BF16)

    def order(index):
        first = floor_div(index, unit)
        rest = index - first * unit
        second = floor_div(rest, part)
        return second * unit + first * part + (rest - second * part)

    perm[...] = one_hot(order(iota_f32((size, 1), 0)) == iota_f32((size, size), 1))
    perm_back[...] = one_hot(iota_f32((size, size), 0) == order(iota_f32((1, size), 1)))
    acc[...] = jnp.zeros_like(acc)

    lag_down = LAG_USE + chunks - 1

    def staged(lag, count=total):
        def wrap(body):
            def run(now):
                @pl.when((now >= lag) & (now < count + lag))
                def _():
                    body(now - lag)
            return run
        return wrap

    def either(test, yes, no):
        if test is None:
            no()
        else:
            pl.when(test)(yes)
            pl.when(jnp.logical_not(test))(no)

    def gather_split(q):
        return lax.rem(q, chunks) >= chunks - split_in if split_in else None

    def scatter_split(p):
        return lax.rem(p, chunks) < split_out if split_out else None

    @staged(-AHEAD)
    def stage_offer(q):
        offer(q)

    @staged(0, chunks)
    def stage_weights(k):
        @pl.when(k + 1 < chunks)
        def _():
            for copy in up_copies(k + 1):
                copy.start()

        for copy in down_copies(k):
            copy.start()

    @staged(0)
    def stage_arrive(q):
        def both():
            arrive_near(q, 0, False)
            arrive_near(q, 1, False)

        either(gather_split(q), both, lambda: arrive_near(q, 0, True))

        @pl.when(q == chunks // 2)
        def _():
            route_local().wait()
            for step in range(1, zs):
                route_z(step).wait_recv()
            route_side(side).start()

    @staged(-SPLIT_AHEAD)
    def stage_split(q):
        def both():
            y_hop(q, other_side, z, 4).wait_recv()
            z_own(q, 1)

        either(gather_split(q), both, lambda: None)

    @staged(LAG_RELAY)
    def stage_relay(q):
        def both():
            arrive_far(q, 0, False)
            arrive_far(q, 1, False)
            core_hop(q, core, 0).start()
            core_hop(q, core, 1).start()

        def one():
            arrive_far(q, 0, True)
            core_hop(q, core, 0).start()

        either(gather_split(q), both, one)

    @staged(LAG_SIDE)
    def stage_side(q):
        def one():
            spot = xb.at[q, core, other_side]
            send(spot, spot, out_s.at[5], ay_r.at[q], side_dev).wait_recv()
            core_hop(q, core, 1).start()

        either(gather_split(q), lambda: None, one)

        @pl.when(q == chunks // 2)
        def _():
            route_side(other_side).wait_recv()
            route_core(core).start()

    @staged(LAG_USE)
    def stage_up(q):
        spot = xb.at[q, other_core]
        send(spot, spot, out_s.at[6], ac_r.at[q], core_dev).wait_recv()
        k = lax.rem(q, chunks)

        @pl.when(q < chunks)
        def _():
            up_wait(k)

        folded = xb[q].reshape(groups, size, CHUNK)
        moved = jnp.dot(perm[...], jnp.concatenate([folded[g] for g in range(groups)], axis=1), preferred_element_type=F32).astype(BF16)
        left = jnp.concatenate([
            jnp.concatenate([moved[f * unit:(f + 1) * unit, g * CHUNK:(g + 1) * CHUNK] for f in range(fold)], axis=1)
            for g in range(groups)
        ], axis=0)
        for e in range(EXP_G):
            acc[2 * e] += jnp.dot(left, wb[k, e], preferred_element_type=F32)
            acc[2 * e + 1] += jnp.dot(left, wb[k, EXP_G + e], preferred_element_type=F32)

        @pl.when(k == max(chunks - 3, chunks // 2))
        def _():
            b = q // chunks

            @pl.when(b == 0)
            def _():
                route_core(other_core).wait_recv()

            line = iota_f32((1, units * pad_rows), 1)
            unit_of = floor_div(line, pad_rows)
            row_of = line - unit_of * pad_rows - (b * part).astype(F32)
            wanted = jnp.where((row_of >= 0) & (row_of < part), unit_of * part + row_of, -1.0)
            pick = one_hot(iota_f32((lines, units * pad_rows), 0) == wanted)
            scales = jnp.dot(pick, rb[...].reshape(units * pad_rows, LANES), preferred_element_type=F32)
            lane = lax.broadcasted_iota(jnp.int32, (lines, LANES), 1)
            first_expert = me // (wide // GROUPS) * EXP_G
            for e in range(EXP_G):
                scale = jnp.sum(jnp.where(lane == first_expert + e, scales, 0.0), axis=1, keepdims=True)
                scale_ref[e] = jnp.broadcast_to(scale, (lines, LANES))

        @pl.when(k == chunks - 1)
        def _():
            b = q // chunks

            for e in range(EXP_G):
                scale = scale_ref[e][:, :1]
                gate = acc[2 * e]
                value = gate / (1.0 + jnp.exp(-gate)) * acc[2 * e + 1]
                hid[b, :, e * hidden:(e + 1) * hidden] = (value * scale).astype(BF16)
            if batches > 1:
                acc[...] = jnp.zeros_like(acc)

    @staged(lag_down)
    def stage_down(p):
        k = lax.rem(p, chunks)

        @pl.when(p < chunks)
        def _():
            down_wait(k)

        down = jnp.dot(hid[p // chunks], wdb[k], preferred_element_type=F32).astype(BF16)
        stacked = jnp.concatenate([
            jnp.concatenate([down[g * unit:(g + 1) * unit, f * CHUNK:(f + 1) * CHUNK] for f in range(fold)], axis=0)
            for g in range(groups)
        ], axis=1)
        moved = jnp.dot(perm_back[...], stacked, preferred_element_type=F32).astype(BF16)
        flat = jnp.concatenate([moved[:, g * CHUNK:(g + 1) * CHUNK] for g in range(groups)], axis=0)
        packed[p] = flat.reshape(CORES, SIDES, zs, unit, CHUNK)
        back_core(p).start()

    @staged(lag_down + LAG_SUM)
    def stage_sum(p):
        back_core(p).wait_recv()
        for rel in (1, 0):
            red[p, rel] = (packed[p, core, halves[rel]].astype(F32) + got_core[p, halves[rel]].astype(F32)).astype(BF16)

        def both():
            reduce_first(p, 0)
            reduce_first(p, 1)

        def one():
            for d, sign, dst, slot in reversed(around(range(1, zs))):
                @pl.when(inside(dst))
                def _():
                    back_side(p, dst).start()

        either(scatter_split(p), both, one)

        @pl.when(p == total - 1)
        def _():
            @pl.loop(0, total)
            def _(j):
                either(scatter_split(j), lambda: None, lambda: back_own(j).start())

    @staged(lag_down + LAG_Z)
    def stage_z(p):
        def both():
            reduce_second(p, 0)
            reduce_second(p, 1)

        def one():
            spot = got_side.at[p, pl.ds(0, zs - 1)]
            send(spot, spot, out_s.at[8], by_r.at[p], side_dev).wait_recv()
            for step in range(1, zs):
                dst = lax.rem(z + step, zs)
                red[p, 0, dst] = (red[p, 0, dst].astype(F32) + got_side[p, dst].astype(F32)).astype(BF16)
            reduce_first(p, 0)

        either(scatter_split(p), both, one)

    @staged(lag_down + LAG_ZR)
    def stage_zr(p):
        def both():
            got_y[p, 0] = reduce_last(p, 1).astype(BF16)
            back_last(p).start()

        either(scatter_split(p), both, lambda: reduce_second(p, 0))

    @staged(lag_down + LAG_END)
    def stage_end(p):
        b = p // chunks
        k = lax.rem(p, chunks)
        spot = pl.ds(pl.multiple_of(b * unit, unit), unit)

        def both():
            back_last(p).wait_recv()
            fin[k, spot] = (reduce_last(p, 0) + got_y[p, 1].astype(F32)).astype(BF16)

        def one():
            back_own(p).wait_recv()
            fin[k, spot] = (reduce_last(p, 0) + got_side[p, z].astype(F32)).astype(BF16)

        either(scatter_split(p), both, one)

        @pl.when(b == batches - 1)
        def _():
            out_of = one_hot(iota_f32((fold * pad_rows, held), 0) == place(iota_f32((1, held), 1)))
            flat = jnp.dot(out_of, fin[k], preferred_element_type=F32).astype(BF16)
            for f in range(fold):
                columns = pl.ds(pl.multiple_of(k * span + f * CHUNK, CHUNK), CHUNK)
                out_v[:, columns] = flat[f * pad_rows:f * pad_rows + rows]
            columns = pl.ds(pl.multiple_of(k * span, span), span)
            pltpu.make_async_copy(out_v.at[:, columns], out_ref.at[:, columns], tok_sem).start()

    @pl.loop(0, total + lag_down + LAG_END)
    def _(now):
        stage_offer(now)
        stage_arrive(now)
        stage_split(now)
        stage_relay(now)
        stage_side(now)
        stage_weights(now)
        stage_sum(now)
        stage_z(now)
        stage_zr(now)
        stage_end(now)
        stage_up(now)
        stage_down(now)

    def sent(kind, spot):
        send(spot, spot, out_s.at[kind], ay_r.at[0], core_dev).wait_send()

    pltpu.make_async_copy(out_v, out_ref, tok_sem).wait()
    def sent_lines(kind, pairs, rule, extra):
        by_count(pairs, rule, lambda n: sent(kind, red.at[:, 0, pl.ds(0, n)]))
        if extra:
            by_count(pairs, rule, lambda n: sent(kind + 1, red.at[pl.ds(0, extra), 0, pl.ds(0, n)]))

    sent_lines(0, ends(near), any_end, extra_in)
    sent_lines(2, ends(range(NEAR, zs - 1)), any_through, extra_in)
    sent(4, red.at[:, 0, 0])
    sent(5, red.at[pl.ds(0, total - extra_in), 0, pl.ds(0, zs - 1)])
    sent(6, xb.at[:, 0])
    sent(7, packed.at[:, 0])
    sent(8, red.at[pl.ds(0, total - extra_out), 0, pl.ds(0, zs - 1)])
    sent(14, red.at[pl.ds(0, total - extra_out), 0, 0])
    sent_lines(10, ends(near), any_end, extra_out)
    sent_lines(12, ends(far), any_end, extra_out)
    if extra_out:
        sent(9, got_y.at[pl.ds(0, extra_out), 0])
    spot = rb.at[0, 0, pl.ds(0, zs - 1)]
    send(spot, spot, route_s.at[0], route_r.at[0], core_dev).wait_send()
    route_side(side).wait_send()
    route_core(core).wait_send()


def local(wide, interpret, tokens, expert_ids, gates, w_gate, w_up, w_down):
    rows, model = tokens.shape
    hidden = w_gate.shape[2]
    batches = BATCHES if rows % BATCHES == 0 else 1
    part = rows // batches
    fold = 16 // math.gcd(16, part)
    span = fold * CHUNK
    chunks = model // span
    total = batches * chunks
    split_in, split_out = min(SPLIT_IN, chunks), min(SPLIT_OUT, chunks)
    extra = batches * max(split_in, split_out)
    zs = wide // (CORES * SIDES)
    pad_rows = -(-rows // 16) * 16
    unit = part * fold
    size = fold * unit
    lines = wide * part
    slots = 2 * min(NEAR, zs - 1)

    any_space = pl.BlockSpec(memory_space=pl.ANY)
    dma = pltpu.SemaphoreType.DMA
    out = pl.pallas_call(
        functools.partial(kernel, wide, rows, batches, fold, split_in, split_out),
        out_shape=jax.ShapeDtypeStruct((rows, model), BF16),
        in_specs=[any_space] + [pl.BlockSpec(memory_space=pltpu.VMEM)] * 2 + [any_space] * 3,
        out_specs=any_space,
        scratch_shapes=[
            pltpu.VMEM((rows, model), BF16),
            pltpu.VMEM((pad_rows, LANES), BF16),
            pltpu.VMEM((total, CORES, SIDES, zs, unit, CHUNK), BF16),
            pltpu.VMEM((CORES, SIDES, zs, pad_rows, LANES), BF16),
            pltpu.VMEM((chunks, 2 * EXP_G, span, hidden), BF16),
            pltpu.VMEM((chunks, EXP_G * hidden, span), BF16),
            pltpu.VMEM((2 * EXP_G, lines, hidden), F32),
            pltpu.VMEM((batches, lines, EXP_G * hidden), BF16),
            pltpu.VMEM((size, size), BF16),
            pltpu.VMEM((size, size), BF16),
            pltpu.VMEM((total, CORES, SIDES, zs, unit, CHUNK), BF16),
            pltpu.VMEM((total, SIDES, zs, unit, CHUNK), BF16),
            pltpu.VMEM((total, SIDES, zs, unit, CHUNK), BF16),
            pltpu.VMEM((total, zs, unit, CHUNK), BF16),
            pltpu.VMEM((total, SIDES, slots, unit, CHUNK), BF16),
            pltpu.VMEM((total if zs - 1 > NEAR else 1, SIDES, zs, unit, CHUNK), BF16),
            pltpu.VMEM((total if split_out else 1, 2, unit, CHUNK), BF16),
            pltpu.VMEM((chunks, batches * unit, CHUNK), BF16),
            pltpu.VMEM((EXP_G, lines, LANES), F32),
            pltpu.VMEM((rows, model), BF16),
            dma(()),
            dma(()),
            dma((chunks,)),
            dma((chunks,)),
            dma((3,)),
            dma((zs + 2,)),
            dma((15,)),
            dma((total + extra, slots)),
            dma((total + extra, zs - 1 - NEAR) if zs - 1 > NEAR else (1, 1)),
            dma((total,)),
            dma((total,)),
            dma((total,)),
            dma((total,)),
            dma((total,)),
            dma((total + extra,)),
            dma((total + extra, zs - 1 - NEAR) if zs - 1 > NEAR else (1, 1)),
        ],
        compiler_params=pltpu.CompilerParams(collective_id=0, has_side_effects=True, vmem_limit_bytes=67043328),
        **interpret,
    )(tokens, expert_ids.T, gates.T, w_gate, w_up, w_down)
    return out


def solution(mesh, interpret=None):
    return jax.shard_map(
        functools.partial(local, mesh.shape["wide"], interpret or {}),
        mesh=mesh,
        in_specs=(
            P(("parts", "wide"), None),
            P(("parts", "wide"), None),
            P(("parts", "wide"), None),
            P(None, None, "wide"),
            P(None, None, "wide"),
            P(None, "wide", None),
        ),
        out_specs=P(("parts", "wide"), None),
        check_vma=False,
    )
```

```python
import functools
import math

import jax
import jax.numpy as jnp
from jax import lax
from jax.experimental import pallas as pl
from jax.experimental.pallas import tpu as pltpu
from jax.sharding import PartitionSpec as P

GROUPS = 8
EXP_G = 2
CORES = 2
SIDES = 2
LANES = 128
CHUNK = 256
BATCHES = 1
SPLIT_IN = 1
SPLIT_OUT = 0
AHEAD = 20
SPLIT_AHEAD = 4
LAG_RELAY = 2
LAG_SIDE = 4
LAG_USE = 5
LAG_SUM = 2
LAG_Z = 4
LAG_ZR = 6
LAG_END = 10
NEAR = 2
F32 = jnp.float32
BF16 = jnp.bfloat16


def floor_div(value, by):
    return jnp.floor((value + 0.5) * (1.0 / by))


def iota_f32(shape, dim):
    return lax.broadcasted_iota(jnp.int32, shape, dim).astype(F32)


def one_hot(match):
    return match.astype(F32).astype(BF16)


def kernel(
    wide, rows, batches, fold, split_in, split_out,
    tok_ref, ids_ref, gate_ref, wg_ref, wu_ref, wd_ref, out_ref,
    tok, r_ref, xb, rb, wb, wdb, acc, hid, perm, perm_back, packed, got_core, red, got_side, got_z, relay, got_y, fin, scale_ref, out_v,
    tok_sem, own_sem, w_sem, d_sem, route_s, route_r, out_s, az_r, af_r, ay_r, ac_r, bc_r, by_r, bo_r, bz_r, br_r,
):
    zs = wide // (CORES * SIDES)
    total = xb.shape[0]
    chunks = total // batches
    hidden = wg_ref.shape[2]
    part = rows // batches
    unit = part * fold
    span = fold * CHUNK
    units = wide
    groups = units // fold
    size = fold * unit
    lines = units * part
    pad_rows = r_ref.shape[0]
    near = range(1, min(NEAR, zs - 1) + 1)
    far = range(NEAR + 1, zs)
    extra_in = batches * split_in
    extra_out = batches * split_out

    me = lax.axis_index("wide")
    core = lax.rem(me, CORES)
    chip = me // CORES
    side = lax.rem(chip, SIDES)
    z = chip // SIDES
    other_core = 1 - core
    other_side = 1 - side
    halves = (side, other_side)

    def at(z_at, side_at, core_at):
        return {"wide": (z_at * SIDES + side_at) * CORES + core_at}

    core_dev = at(z, side, other_core)
    side_dev = at(z, other_side, core)

    def inside(value):
        return (value >= 0) & (value < zs)

    def around(distances):
        return [(d, sign, z + sign * d, (d - 1) * 2 + (sign + 1) // 2) for d in distances for sign in (-1, 1)]

    def send(src, dst, s_sem, r_sem, dev):
        return pltpu.make_async_remote_copy(
            src_ref=src, dst_ref=dst, send_sem=s_sem, recv_sem=r_sem, device_id=dev, device_id_type=pl.DeviceIdType.MESH
        )

    def up_copies(k):
        rows_of = pl.ds(pl.multiple_of(k * span, span), span)
        return [
            pltpu.make_async_copy(wg_ref.at[:, rows_of, :], wb.at[k, pl.ds(0, EXP_G)], w_sem.at[k]),
            pltpu.make_async_copy(wu_ref.at[:, rows_of, :], wb.at[k, pl.ds(EXP_G, EXP_G)], w_sem.at[k]),
        ]

    def up_wait(k):
        pltpu.make_async_copy(wb.at[k], wb.at[k], w_sem.at[k]).wait()

    def down_copies(k):
        columns = pl.ds(pl.multiple_of(k * span, span), span)
        return [
            pltpu.make_async_copy(wd_ref.at[e, :, columns], wdb.at[k, pl.ds(e * hidden, hidden), :], d_sem.at[k])
            for e in range(EXP_G)
        ]

    def down_wait(k):
        pltpu.make_async_copy(wdb.at[k], wdb.at[k], d_sem.at[k]).wait()

    def line_in(q, rel):
        return q if rel == 0 else total + q // chunks * split_in + lax.rem(q, chunks) - (chunks - split_in)

    def line_out(p, rel):
        return p if rel == 0 else total + p // chunks * split_out + lax.rem(p, chunks)

    def by_count(pairs, rule, act):
        here = sum(rule(z + sign * d, z - sign).astype(jnp.int32) for d, sign in pairs)
        held_here = {sum(bool(rule(spot + sign * d, spot - sign)) for d, sign in pairs) for spot in range(zs)}
        for n in sorted(held_here - {0}):
            @pl.when(here == n)
            def _():
                act(n)

    def ends(distances):
        return [(d, sign) for d in distances for sign in (-1, 1)]

    def any_end(value, behind):
        return inside(value)

    def any_through(value, behind):
        return inside(value) & inside(behind)

    def any_first(value, behind):
        return inside(value) & ((behind < 0) | (behind >= zs))

    def z_hop(q, rel, src, dst, kind, r_sem):
        spot = xb.at[q, core, halves[rel], src]
        return send(spot, spot, out_s.at[kind], r_sem, at(dst, side, core))

    def y_hop(q, half, src, kind):
        spot = xb.at[q, core, half, src]
        return send(spot, spot, out_s.at[kind], ay_r.at[q], side_dev)

    def core_hop(q, owner, rel):
        spot = xb.at[q, owner, halves[rel]]
        return send(spot, spot, out_s.at[6], ac_r.at[q], core_dev)

    def z_own(q, rel):
        line = line_in(q, rel)
        for d, sign, dst, slot in reversed(around(near)):
            @pl.when(inside(dst))
            def _():
                z_hop(q, rel, z, dst, rel, az_r.at[line]).start()

    def z_onward(q, rel, distances, onward):
        for d, sign, src, slot in around(distances):
            @pl.when(inside(src))
            def _():
                if d >= NEAR and d + 1 < zs:
                    @pl.when(inside(z - sign))
                    def _():
                        z_hop(q, rel, src, z - sign, 2 + rel, af_r.at[line_in(q, rel), d - NEAR]).start()
                if onward:
                    y_hop(q, side, src, 5).start()

    def z_wait(q, rel, distances, r_sem):
        def wait(n):
            spot = xb.at[q, core, halves[rel], pl.ds(0, n)]
            send(spot, spot, out_s.at[0], r_sem, core_dev).wait_recv()

        by_count(ends(distances), any_end, wait)

    def arrive_near(q, rel, onward):
        z_wait(q, rel, near, az_r.at[line_in(q, rel)])
        z_onward(q, rel, near, onward)

    def arrive_far(q, rel, onward):
        for d in far:
            z_wait(q, rel, [d], af_r.at[line_in(q, rel), d - NEAR - 1])
            z_onward(q, rel, [d], onward)

    def route_z(step):
        dst = lax.rem(z + step, zs)
        return send(r_ref, rb.at[core, side, z], route_s.at[0], route_r.at[step], at(dst, side, core))

    def route_side(half):
        return send(rb.at[core, half], rb.at[core, half], route_s.at[1], route_r.at[zs], side_dev)

    def route_core(owner):
        return send(rb.at[owner], rb.at[owner], route_s.at[2], route_r.at[zs + 1], core_dev)

    def route_local():
        return pltpu.make_async_copy(r_ref, rb.at[core, side, z], own_sem)

    def back_core(p):
        return send(packed.at[p, other_core], got_core.at[p], out_s.at[7], bc_r.at[p], core_dev)

    def back_side(p, dst):
        return send(red.at[p, 1, dst], got_side.at[p, dst], out_s.at[8], by_r.at[p], side_dev)

    def back_own(p):
        return send(red.at[p, 1, z], got_side.at[p, z], out_s.at[14], bo_r, side_dev)

    def back_last(p):
        return send(got_y.at[p, 0], got_y.at[p, 1], out_s.at[9], by_r.at[p], side_dev)

    def back_z(p, rel, dst, slot):
        r_sem = bz_r.at[line_out(p, rel)]
        return send(red.at[p, rel, dst], got_z.at[p, rel, slot], out_s.at[10 + rel], r_sem, at(dst, side, core))

    def back_relay(p, rel, d, dst, to):
        r_sem = br_r.at[line_out(p, rel), d]
        return send(red.at[p, rel, dst], relay.at[p, rel, dst], out_s.at[12 + rel], r_sem, at(to, side, core))

    def reduce_out(p, rel, d, sign, dst, slot):
        if d <= NEAR:
            back_z(p, rel, dst, slot).start()
        else:
            back_relay(p, rel, d - NEAR - 1, dst, z + sign).start()

    def reduce_first(p, rel):
        for d, sign, dst, slot in reversed(around(range(1, zs))):
            ready = inside(dst) if d < NEAR else any_first(dst, z - sign)

            @pl.when(ready)
            def _():
                reduce_out(p, rel, d, sign, dst, slot)

    def reduce_second(p, rel):
        for d in reversed(range(NEAR, zs - 1)):
            def wait(n):
                spot = relay.at[p, rel, pl.ds(0, n)]
                send(spot, spot, out_s.at[0], br_r.at[line_out(p, rel), d - NEAR], core_dev).wait_recv()

            by_count(ends([d]), any_through, wait)
            for _, sign, dst, slot in around([d]):
                @pl.when(any_through(dst, z - sign))
                def _():
                    red[p, rel, dst] = (red[p, rel, dst].astype(F32) + relay[p, rel, dst].astype(F32)).astype(BF16)
                    reduce_out(p, rel, d, sign, dst, slot)

    def reduce_last(p, rel):
        def wait(n):
            spot = got_z.at[p, rel, pl.ds(0, n)]
            send(spot, spot, out_s.at[0], bz_r.at[line_out(p, rel)], core_dev).wait_recv()

        by_count(ends(near), any_end, wait)
        done = red[p, rel, z].astype(F32)
        for d, sign, src, slot in around(near):
            done = done + got_z[p, rel, slot].astype(F32)
        return done

    token_copy = pltpu.make_async_copy(tok_ref, tok, tok_sem)
    token_copy.start()
    for copy in up_copies(0):
        copy.start()

    barrier = pltpu.get_barrier_semaphore()
    for step in range(1, zs):
        pl.semaphore_signal(barrier, inc=1, device_id=at(lax.rem(z + step, zs), side, core), device_id_type=pl.DeviceIdType.MESH)
    pl.semaphore_signal(barrier, inc=1, device_id=side_dev, device_id_type=pl.DeviceIdType.MESH)
    pl.semaphore_signal(barrier, inc=1, device_id=core_dev, device_id_type=pl.DeviceIdType.MESH)

    def place(index):
        batch = floor_div(index, unit)
        rest = index - batch * unit
        block = floor_div(rest, part)
        return block * pad_rows + batch * part + rest - block * part

    held = batches * unit
    into = one_hot(iota_f32((held, fold * pad_rows), 1) == place(iota_f32((held, 1), 0)))
    spread = one_hot(iota_f32((pad_rows, rows), 0) == iota_f32((pad_rows, rows), 1))
    token = lax.broadcasted_iota(jnp.int32, (LANES, rows), 0)
    route = jnp.zeros((LANES, rows), F32)
    for slot in range(ids_ref.shape[0]):
        route = route + jnp.where(ids_ref[slot:slot + 1, :] == token, gate_ref[slot:slot + 1, :], 0.0)
    r_ref[...] = lax.dot_general(spread, route.astype(BF16), (((1,), (1,)), ((), ())), preferred_element_type=F32).astype(BF16)
    route_local().start()
    token_copy.wait()

    def pack(k):
        padded = jnp.dot(spread, tok[:, k * span:(k + 1) * span], preferred_element_type=F32).astype(BF16)
        tiles = jnp.concatenate([padded[:, f * CHUNK:(f + 1) * CHUNK] for f in range(fold)], axis=0)
        mine = jnp.dot(into, tiles, preferred_element_type=F32).astype(BF16)
        for b in range(batches):
            xb[b * chunks + k, core, side, z] = mine[b * unit:(b + 1) * unit]

    def offer(q):
        y_hop(q, side, z, 4).start()
        z_own(q, 0)

    pack(0)
    pl.semaphore_wait(barrier, zs + 1)
    offer(0)
    for step in range(1, zs):
        route_z(step).start()
    for k in range(1, chunks):
        pack(k)
        if k < AHEAD:
            offer(k)
    for q in range(chunks, min(AHEAD, total)):
        offer(q)

    for d, sign, src, slot in around(near):
        @pl.when(jnp.logical_not(inside(z - sign * d)))
        def _():
            @pl.loop(0, total)
            def _(p):
                for rel in range(SIDES if split_out else 1):
                    got_z[p, rel, slot] = jnp.zeros((unit, CHUNK), BF16)

    def order(index):
        first = floor_div(index, unit)
        rest = index - first * unit
        second = floor_div(rest, part)
        return second * unit + first * part + (rest - second * part)

    perm[...] = one_hot(order(iota_f32((size, 1), 0)) == iota_f32((size, size), 1))
    perm_back[...] = one_hot(iota_f32((size, size), 0) == order(iota_f32((1, size), 1)))
    acc[...] = jnp.zeros_like(acc)

    lag_down = LAG_USE + chunks - 1

    def staged(lag, count=total):
        def wrap(body):
            def run(now):
                @pl.when((now >= lag) & (now < count + lag))
                def _():
                    body(now - lag)
            return run
        return wrap

    def either(test, yes, no):
        if test is None:
            no()
        else:
            pl.when(test)(yes)
            pl.when(jnp.logical_not(test))(no)

    def gather_split(q):
        return lax.rem(q, chunks) >= chunks - split_in if split_in else None

    def scatter_split(p):
        return lax.rem(p, chunks) < split_out if split_out else None

    @staged(-AHEAD)
    def stage_offer(q):
        offer(q)

    @staged(0, chunks)
    def stage_weights(k):
        @pl.when(k + 1 < chunks)
        def _():
            for copy in up_copies(k + 1):
                copy.start()

        for copy in down_copies(k):
            copy.start()

    @staged(0)
    def stage_arrive(q):
        def both():
            arrive_near(q, 0, False)
            arrive_near(q, 1, False)

        either(gather_split(q), both, lambda: arrive_near(q, 0, True))

        @pl.when(q == chunks // 2)
        def _():
            route_local().wait()
            for step in range(1, zs):
                route_z(step).wait_recv()
            route_side(side).start()

    @staged(-SPLIT_AHEAD)
    def stage_split(q):
        def both():
            y_hop(q, other_side, z, 4).wait_recv()
            z_own(q, 1)

        either(gather_split(q), both, lambda: None)

    @staged(LAG_RELAY)
    def stage_relay(q):
        def both():
            arrive_far(q, 0, False)
            arrive_far(q, 1, False)
            core_hop(q, core, 0).start()
            core_hop(q, core, 1).start()

        def one():
            arrive_far(q, 0, True)
            core_hop(q, core, 0).start()

        either(gather_split(q), both, one)

    @staged(LAG_SIDE)
    def stage_side(q):
        def one():
            spot = xb.at[q, core, other_side]
            send(spot, spot, out_s.at[5], ay_r.at[q], side_dev).wait_recv()
            core_hop(q, core, 1).start()

        either(gather_split(q), lambda: None, one)

        @pl.when(q == chunks // 2)
        def _():
            route_side(other_side).wait_recv()
            route_core(core).start()

    @staged(LAG_USE)
    def stage_up(q):
        spot = xb.at[q, other_core]
        send(spot, spot, out_s.at[6], ac_r.at[q], core_dev).wait_recv()
        k = lax.rem(q, chunks)

        @pl.when(q < chunks)
        def _():
            up_wait(k)

        folded = xb[q].reshape(groups, size, CHUNK)
        moved = jnp.dot(perm[...], jnp.concatenate([folded[g] for g in range(groups)], axis=1), preferred_element_type=F32).astype(BF16)
        left = jnp.concatenate([
            jnp.concatenate([moved[f * unit:(f + 1) * unit, g * CHUNK:(g + 1) * CHUNK] for f in range(fold)], axis=1)
            for g in range(groups)
        ], axis=0)
        for e in range(EXP_G):
            acc[2 * e] += jnp.dot(left, wb[k, e], preferred_element_type=F32)
            acc[2 * e + 1] += jnp.dot(left, wb[k, EXP_G + e], preferred_element_type=F32)

        @pl.when(k == max(chunks - 3, chunks // 2))
        def _():
            b = q // chunks

            @pl.when(b == 0)
            def _():
                route_core(other_core).wait_recv()

            line = iota_f32((1, units * pad_rows), 1)
            unit_of = floor_div(line, pad_rows)
            row_of = line - unit_of * pad_rows - (b * part).astype(F32)
            wanted = jnp.where((row_of >= 0) & (row_of < part), unit_of * part + row_of, -1.0)
            pick = one_hot(iota_f32((lines, units * pad_rows), 0) == wanted)
            scales = jnp.dot(pick, rb[...].reshape(units * pad_rows, LANES), preferred_element_type=F32)
            lane = lax.broadcasted_iota(jnp.int32, (lines, LANES), 1)
            first_expert = me // (wide // GROUPS) * EXP_G
            for e in range(EXP_G):
                scale = jnp.sum(jnp.where(lane == first_expert + e, scales, 0.0), axis=1, keepdims=True)
                scale_ref[e] = jnp.broadcast_to(scale, (lines, LANES))

        @pl.when(k == chunks - 1)
        def _():
            b = q // chunks

            for e in range(EXP_G):
                scale = scale_ref[e][:, :1]
                gate = acc[2 * e]
                value = gate / (1.0 + jnp.exp(-gate)) * acc[2 * e + 1]
                hid[b, :, e * hidden:(e + 1) * hidden] = (value * scale).astype(BF16)
            if batches > 1:
                acc[...] = jnp.zeros_like(acc)

    @staged(lag_down)
    def stage_down(p):
        k = lax.rem(p, chunks)

        @pl.when(p < chunks)
        def _():
            down_wait(k)

        down = jnp.dot(hid[p // chunks], wdb[k], preferred_element_type=F32).astype(BF16)
        stacked = jnp.concatenate([
            jnp.concatenate([down[g * unit:(g + 1) * unit, f * CHUNK:(f + 1) * CHUNK] for f in range(fold)], axis=0)
            for g in range(groups)
        ], axis=1)
        moved = jnp.dot(perm_back[...], stacked, preferred_element_type=F32).astype(BF16)
        flat = jnp.concatenate([moved[:, g * CHUNK:(g + 1) * CHUNK] for g in range(groups)], axis=0)
        packed[p] = flat.reshape(CORES, SIDES, zs, unit, CHUNK)
        back_core(p).start()

    @staged(lag_down + LAG_SUM)
    def stage_sum(p):
        back_core(p).wait_recv()
        for rel in (1, 0):
            red[p, rel] = (packed[p, core, halves[rel]].astype(F32) + got_core[p, halves[rel]].astype(F32)).astype(BF16)

        def both():
            reduce_first(p, 0)
            reduce_first(p, 1)

        def one():
            for d, sign, dst, slot in reversed(around(range(1, zs))):
                @pl.when(inside(dst))
                def _():
                    back_side(p, dst).start()

        either(scatter_split(p), both, one)

        @pl.when(p == total - 1)
        def _():
            @pl.loop(0, total)
            def _(j):
                either(scatter_split(j), lambda: None, lambda: back_own(j).start())

    @staged(lag_down + LAG_Z)
    def stage_z(p):
        def both():
            reduce_second(p, 0)
            reduce_second(p, 1)

        def one():
            spot = got_side.at[p, pl.ds(0, zs - 1)]
            send(spot, spot, out_s.at[8], by_r.at[p], side_dev).wait_recv()
            for step in range(1, zs):
                dst = lax.rem(z + step, zs)
                red[p, 0, dst] = (red[p, 0, dst].astype(F32) + got_side[p, dst].astype(F32)).astype(BF16)
            reduce_first(p, 0)

        either(scatter_split(p), both, one)

    @staged(lag_down + LAG_ZR)
    def stage_zr(p):
        def both():
            got_y[p, 0] = reduce_last(p, 1).astype(BF16)
            back_last(p).start()

        either(scatter_split(p), both, lambda: reduce_second(p, 0))

    @staged(lag_down + LAG_END)
    def stage_end(p):
        @pl.when(p == 0)
        def _():
            spot = got_side.at[pl.ds(0, total - extra_out), 0]
            send(spot, spot, out_s.at[14], bo_r, side_dev).wait_recv()

        b = p // chunks
        k = lax.rem(p, chunks)
        spot = pl.ds(pl.multiple_of(b * unit, unit), unit)

        def both():
            back_last(p).wait_recv()
            fin[k, spot] = (reduce_last(p, 0) + got_y[p, 1].astype(F32)).astype(BF16)

        def one():
            fin[k, spot] = (reduce_last(p, 0) + got_side[p, z].astype(F32)).astype(BF16)

        either(scatter_split(p), both, one)

        @pl.when(b == batches - 1)
        def _():
            out_of = one_hot(iota_f32((fold * pad_rows, held), 0) == place(iota_f32((1, held), 1)))
            flat = jnp.dot(out_of, fin[k], preferred_element_type=F32).astype(BF16)
            for f in range(fold):
                columns = pl.ds(pl.multiple_of(k * span + f * CHUNK, CHUNK), CHUNK)
                out_v[:, columns] = flat[f * pad_rows:f * pad_rows + rows]
            columns = pl.ds(pl.multiple_of(k * span, span), span)
            pltpu.make_async_copy(out_v.at[:, columns], out_ref.at[:, columns], tok_sem).start()

    @pl.loop(0, total + lag_down + LAG_END)
    def _(now):
        stage_offer(now)
        stage_arrive(now)
        stage_split(now)
        stage_relay(now)
        stage_side(now)
        stage_weights(now)
        stage_sum(now)
        stage_z(now)
        stage_zr(now)
        stage_up(now)
        stage_down(now)
        stage_end(now)

    def sent(kind, spot):
        send(spot, spot, out_s.at[kind], ay_r.at[0], core_dev).wait_send()

    pltpu.make_async_copy(out_v, out_ref, tok_sem).wait()
    def sent_lines(kind, pairs, rule, extra):
        by_count(pairs, rule, lambda n: sent(kind, red.at[:, 0, pl.ds(0, n)]))
        if extra:
            by_count(pairs, rule, lambda n: sent(kind + 1, red.at[pl.ds(0, extra), 0, pl.ds(0, n)]))

    sent_lines(0, ends(near), any_end, extra_in)
    sent_lines(2, ends(range(NEAR, zs - 1)), any_through, extra_in)
    sent(4, red.at[:, 0, 0])
    sent(5, red.at[pl.ds(0, total - extra_in), 0, pl.ds(0, zs - 1)])
    sent(6, xb.at[:, 0])
    sent(7, packed.at[:, 0])
    sent(8, red.at[pl.ds(0, total - extra_out), 0, pl.ds(0, zs - 1)])
    sent(14, red.at[pl.ds(0, total - extra_out), 0, 0])
    sent_lines(10, ends(near), any_end, extra_out)
    sent_lines(12, ends(far), any_end, extra_out)
    if extra_out:
        sent(9, got_y.at[pl.ds(0, extra_out), 0])
    spot = rb.at[0, 0, pl.ds(0, zs - 1)]
    send(spot, spot, route_s.at[0], route_r.at[0], core_dev).wait_send()
    route_side(side).wait_send()
    route_core(core).wait_send()


def local(wide, interpret, tokens, expert_ids, gates, w_gate, w_up, w_down):
    rows, model = tokens.shape
    hidden = w_gate.shape[2]
    batches = BATCHES if rows % BATCHES == 0 else 1
    part = rows // batches
    fold = 16 // math.gcd(16, part)
    span = fold * CHUNK
    chunks = model // span
    total = batches * chunks
    split_in, split_out = min(SPLIT_IN, chunks), min(SPLIT_OUT, chunks)
    extra = batches * max(split_in, split_out)
    zs = wide // (CORES * SIDES)
    pad_rows = -(-rows // 16) * 16
    unit = part * fold
    size = fold * unit
    lines = wide * part
    slots = 2 * min(NEAR, zs - 1)

    any_space = pl.BlockSpec(memory_space=pl.ANY)
    dma = pltpu.SemaphoreType.DMA
    out = pl.pallas_call(
        functools.partial(kernel, wide, rows, batches, fold, split_in, split_out),
        out_shape=jax.ShapeDtypeStruct((rows, model), BF16),
        in_specs=[any_space] + [pl.BlockSpec(memory_space=pltpu.VMEM)] * 2 + [any_space] * 3,
        out_specs=any_space,
        scratch_shapes=[
            pltpu.VMEM((rows, model), BF16),
            pltpu.VMEM((pad_rows, LANES), BF16),
            pltpu.VMEM((total, CORES, SIDES, zs, unit, CHUNK), BF16),
            pltpu.VMEM((CORES, SIDES, zs, pad_rows, LANES), BF16),
            pltpu.VMEM((chunks, 2 * EXP_G, span, hidden), BF16),
            pltpu.VMEM((chunks, EXP_G * hidden, span), BF16),
            pltpu.VMEM((2 * EXP_G, lines, hidden), F32),
            pltpu.VMEM((batches, lines, EXP_G * hidden), BF16),
            pltpu.VMEM((size, size), BF16),
            pltpu.VMEM((size, size), BF16),
            pltpu.VMEM((total, CORES, SIDES, zs, unit, CHUNK), BF16),
            pltpu.VMEM((total, SIDES, zs, unit, CHUNK), BF16),
            pltpu.VMEM((total, SIDES, zs, unit, CHUNK), BF16),
            pltpu.VMEM((total, zs, unit, CHUNK), BF16),
            pltpu.VMEM((total, SIDES, slots, unit, CHUNK), BF16),
            pltpu.VMEM((total if zs - 1 > NEAR else 1, SIDES, zs, unit, CHUNK), BF16),
            pltpu.VMEM((total if split_out else 1, 2, unit, CHUNK), BF16),
            pltpu.VMEM((chunks, batches * unit, CHUNK), BF16),
            pltpu.VMEM((EXP_G, lines, LANES), F32),
            pltpu.VMEM((rows, model), BF16),
            dma(()),
            dma(()),
            dma((chunks,)),
            dma((chunks,)),
            dma((3,)),
            dma((zs + 2,)),
            dma((15,)),
            dma((total + extra,)),
            dma((total + extra, zs - 1 - NEAR) if zs - 1 > NEAR else (1, 1)),
            dma((total,)),
            dma((total,)),
            dma((total,)),
            dma((total,)),
            dma(()),
            dma((total + extra,)),
            dma((total + extra, zs - 1 - NEAR) if zs - 1 > NEAR else (1, 1)),
        ],
        compiler_params=pltpu.CompilerParams(collective_id=0, has_side_effects=True, vmem_limit_bytes=67043328),
        **interpret,
    )(tokens, expert_ids.T, gates.T, w_gate, w_up, w_down)
    return out


def solution(mesh, interpret=None):
    return jax.shard_map(
        functools.partial(local, mesh.shape["wide"], interpret or {}),
        mesh=mesh,
        in_specs=(
            P(("parts", "wide"), None),
            P(("parts", "wide"), None),
            P(("parts", "wide"), None),
            P(None, None, "wide"),
            P(None, None, "wide"),
            P(None, "wide", None),
        ),
        out_specs=P(("parts", "wide"), None),
        check_vma=False,
    )
```
